32 devices in a mesh: groups: 2 (over y), scanx: 4 (over z), scany: 2 (over x), pos: 2 (over core).
Axes of the slice: x: 2, y: 2, z: 4, core: 2. Of those that a mesh axis runs over, the one named last changes fastest.
Arguments:
- specimen: float32 [2, 2048, 512], P(None, ('groups', 'scanx'), 'scany'), parts along dimension 1, may hold values from -5 to 5
- probe_wave: float32 [2, 512, 256], P(None, 'groups'), parts along dimension 1, may hold values from -6 to 6
- amplitudes: bfloat16 [64, 256, 256], P(('groups', 'scanx', 'scany', 'pos')), parts along dimension 0, may hold values from 0 to 2
- offsets: int32 [64, 2], P(('groups', 'scanx', 'scany', 'pos')), parts along dimension 0, may hold values from 0 to 255
Outputs:
- new_specimen: float32 [2, 2048, 512], P(None, ('groups', 'scanx'), 'scany'), parts along dimension 1
- new_probe: float32 [2, 512, 256], P(None, 'groups'), parts along dimension 1
The draws below stay inside these ranges and needn't reach their ends.
There are 2 independent parts, one for each index of `groups`. The reference program is written for one: setup_inputs(seed, part) draws one part's arguments, and reference() takes and returns one part's arrays. A program takes and returns all parts, laid end to end along the dimension named above; each array names one. Nothing has to cross between parts.
Inputs may be any that keep to these rules, and one draw needn't show every extreme that they name: offsets are pixels from the top-left corner of the position's tile.
All inputs are finite; a program needn't handle non-finite values.
Results may differ from the reference program's by a relative error of at most 0.002.
The reference program's roundings to bfloat16 on the way count: a program that leaves them out, or rounds other values in their place, can miss the bound.
Values sent between devices are 32-bit elements; how exact they have to be, the bound alone decides.
A program may use at most 64 MiB of HBM per device.

```python
import math
import jax
import jax.numpy as jnp
from jax import lax

M = 256
TILE = 256
PER_TILE = 4
TILES_Y = 2
POSITIONS = 32
NXO = 1024
NYO = 512


def place_ends(drawn, stream_key, low, largest):
    index_at = [jax.random.randint(jax.random.fold_in(stream_key, axis), (), 0, length) for axis, length in enumerate(drawn.shape)]
    longest = drawn.shape.index(max(drawn.shape))
    neighbour = index_at[:longest] + [(index_at[longest] + 1) % drawn.shape[longest]] + index_at[longest + 1:]
    return drawn.at[tuple(index_at)].set(low).at[tuple(neighbour)].set(largest)


def level_of(rng, extent, pieces, smallest, largest):
    factor_of = 1.0
    for axis_at, shards_of in pieces:
        steps = jax.random.uniform(jax.random.fold_in(jax.random.fold_in(rng, 6), axis_at), (shards_of,), jnp.float32, smallest / len(pieces), largest / len(pieces))
        factor_of = factor_of * jnp.repeat(jnp.exp(steps), extent[axis_at] // shards_of).reshape((-1,) + (1,) * (len(extent) - 1 - axis_at))
    return factor_of


def noise(stream_key, extent, scale, limit, cuts=(), kind=jnp.bfloat16):
    result = scale * jax.random.normal(stream_key, extent, jnp.float32)
    if cuts:
        result = result * level_of(stream_key, extent, cuts, -0.22, 0.18)
    return jnp.clip(result, -limit, limit).astype(kind)


def setup_inputs(seed: int = 0, part: int = 0) -> dict:
    arg_keys = jax.random.split(jax.random.key(seed), 5)
    part_splits = jax.random.split(jax.random.fold_in(arg_keys[4], part), 5)
    specimen = noise(part_splits[0], (2, NXO, NYO), 0.7, 5.0, ((1, 4), (2, 2)), jnp.float32)
    probe_wave = noise(part_splits[1], (2, M, M), 1.0, 6.0, (), jnp.float32)
    amplitudes = jnp.clip(2.0 * jax.random.uniform(part_splits[2], (POSITIONS, M, M), jnp.float32) ** level_of(part_splits[2], (POSITIONS, M, M), ((0, 16),), -0.2, 0.2), 0.0, 2.0).astype(jnp.bfloat16)
    offsets = place_ends(jax.random.randint(part_splits[3], (POSITIONS, 2), 0, TILE), jax.random.fold_in(part_splits[3], 1), 0, TILE - 1).astype(jnp.int32)
    return dict(specimen=specimen, probe_wave=probe_wave, amplitudes=amplitudes, offsets=offsets)


def dft_tables(length):
    positions_index = jnp.arange(length, dtype=jnp.int32)
    phase_index = positions_index[:, None] * positions_index[None, :] % length
    angle_rad = phase_index.astype(jnp.float32) * (2.0 * math.pi / length)
    scale_factor = 1.0 / math.sqrt(length)
    cosine = (jnp.cos(angle_rad) * scale_factor).astype(jnp.bfloat16)
    sine_part = (jnp.sin(angle_rad) * scale_factor).astype(jnp.bfloat16)
    forward_left = jnp.stack([jnp.stack([cosine, sine_part], 1), jnp.stack([-sine_part, cosine], 1)], 0)
    forward_right = jnp.stack([jnp.stack([cosine, -sine_part], 1), jnp.stack([sine_part, cosine], 1)], 0)
    inverse_left = jnp.stack([jnp.stack([cosine, -sine_part], 1), jnp.stack([sine_part, cosine], 1)], 0)
    inverse_right = jnp.stack([jnp.stack([cosine, sine_part], 1), jnp.stack([-sine_part, cosine], 1)], 0)
    return (forward_left, forward_right, inverse_left, inverse_right)

def left_product(matrix, field_in):
    return jnp.einsum('akbr,brv->akv', matrix.astype(jnp.float32), field_in.astype(jnp.float32))

def right_product(field_in, matrix):
    return jnp.einsum('bkv,bval->akl', field_in.astype(jnp.float32), matrix.astype(jnp.float32))

def project_exit(patch_wave, probe_real, probe_imag, amplitude, tables):
    forward_left, forward_right, inverse_left, inverse_right = tables
    patch_real = patch_wave[0]
    patch_imag = patch_wave[1]
    exit_real = probe_real * patch_real - probe_imag * patch_imag
    exit_imag = probe_real * patch_imag + probe_imag * patch_real
    exit_wave = jnp.stack([exit_real, exit_imag]).astype(jnp.bfloat16)
    half_done = left_product(forward_left, exit_wave).astype(jnp.bfloat16)
    far_field = right_product(half_done, forward_right)
    magnitude = jnp.sqrt(far_field[0] * far_field[0] + far_field[1] * far_field[1])
    scale_ratio = amplitude.astype(jnp.float32) / jnp.maximum(magnitude, 0.2)
    projected = (far_field * scale_ratio[None]).astype(jnp.bfloat16)
    back_half = left_product(inverse_left, projected).astype(jnp.bfloat16)
    back_wave = right_product(back_half, inverse_right)
    return (back_wave[0] - exit_real, back_wave[1] - exit_imag, patch_real, patch_imag)

def reference(specimen, probe_wave, amplitudes, offsets):
    margin = M // 2
    tables = dft_tables(M)
    padded = jnp.pad(specimen, ((0, 0), (margin, margin), (margin, margin)))
    probe_real = probe_wave[0]
    probe_imag = probe_wave[1]
    probe_power = probe_real * probe_real + probe_imag * probe_imag
    tile_index = jnp.arange(POSITIONS, dtype=jnp.int32) // PER_TILE
    tile_row = tile_index // TILES_Y
    tile_col = tile_index % TILES_Y
    row_starts = (tile_row * TILE + offsets[:, 0]).astype(jnp.int32)
    col_starts = (tile_col * TILE + offsets[:, 1]).astype(jnp.int32)
    zero_index = jnp.zeros((), jnp.int32)

    def visit_position(carried, inputs):
        object_grad, probe_grad = carried
        amplitude, row_start, col_start = inputs
        patch_wave = lax.dynamic_slice(padded, (zero_index, row_start, col_start), (2, M, M))
        diff_real, diff_imag, patch_real, patch_imag = project_exit(patch_wave, probe_real, probe_imag, amplitude, tables)
        object_term = jnp.stack([probe_real * diff_real + probe_imag * diff_imag, probe_real * diff_imag - probe_imag * diff_real, probe_power])
        current = lax.dynamic_slice(object_grad, (zero_index, row_start, col_start), (3, M, M))
        object_grad = lax.dynamic_update_slice(object_grad, current + object_term, (zero_index, row_start, col_start))
        probe_term = jnp.stack([patch_real * diff_real + patch_imag * diff_imag, patch_real * diff_imag - patch_imag * diff_real])
        return ((object_grad, probe_grad + probe_term), None)
    start_grad = jnp.zeros((3, NXO + M, NYO + M), jnp.float32)
    start_probe = jnp.zeros((2, M, M), jnp.float32)
    (object_grad, probe_grad), unused = lax.scan(visit_position, (start_grad, start_probe), (amplitudes, row_starts, col_starts))
    core_sum = object_grad[:, margin:margin + NXO, margin:margin + NYO]
    new_specimen = specimen + core_sum[0:2] / (core_sum[2:3] + 1.0)
    step_size = 1.0 / math.sqrt(POSITIONS)
    new_probe = probe_wave + probe_grad * step_size
    return (new_specimen, new_probe)
```

```python
import functools
import math

import jax
import jax.numpy as jnp
import numpy as np
from jax import lax
from jax.experimental import pallas as pl
from jax.experimental.pallas import tpu as pltpu
from jax.sharding import PartitionSpec as P

MESH = pl.DeviceIdType.MESH
VMEM = pltpu.VMEM


def remote(src, dst, send, recv, where):
    return pltpu.make_async_remote_copy(
        src_ref=src, dst_ref=dst, send_sem=send, recv_sem=recv, device_id=where, device_id_type=MESH
    )


def greet(conditions_devices):
    barrier = pltpu.get_barrier_semaphore()
    for present, where in conditions_devices:
        if present is True:
            pl.semaphore_signal(barrier, inc=1, device_id=where, device_id_type=MESH)
        else:

            @pl.when(present)
            def _(where=where):
                pl.semaphore_signal(barrier, inc=1, device_id=where, device_id_type=MESH)

    fixed = sum(1 for present, _ in conditions_devices if present is True)
    peers = [present.astype(jnp.int32) for present, _ in conditions_devices if present is not True]
    pl.semaphore_wait(barrier, sum(peers, fixed))


class Side:
    def __init__(self, axis, count, step):
        me = lax.axis_index(axis)
        self.has = me > 0 if step < 0 else me < count - 1
        self.where = {axis: me + step}


def halo_kernel(nx, ny, spec, pad, send, recv):
    tile = spec.shape[1]
    half = (pad.shape[1] - tile) // 2
    p = lax.axis_index("pos")
    partner = {"pos": 1 - p}
    up, down = Side("scanx", nx, -1), Side("scanx", nx, 1)
    left, right = Side("scany", ny, -1), Side("scany", ny, 1)
    greet([(True, partner)] + [(s.has, s.where) for s in (up, down, left, right)])
    own = pl.ds(half, tile)
    low, high = pl.ds(0, half), pl.ds(half + tile, half)
    every = pl.ds(0, tile + 2 * half)
    first, last = pl.ds(half, half), pl.ds(tile, half)

    def role(q, sides1, sides2, rows_first):
        def at1(piece):
            return (q, piece, own) if rows_first else (q, own, piece)

        def at2(piece):
            return (q, every, piece) if rows_first else (q, piece, every)

        def src1(k):
            piece = pl.ds(0, half) if k == 0 else pl.ds(tile - half, half)
            return spec.at[q, piece, :] if rows_first else spec.at[q, :, piece]

        copies1 = [
            remote(src1(k), pad.at[at1(high if k == 0 else low)], send.at[k], recv.at[k], sides1[k].where)
            for k in range(2)
        ]
        for k in range(2):
            pl.when(sides1[k].has)(copies1[k].start)
        pad[:, own, own] = spec[...]
        for k in range(2):
            mine = low if k == 0 else high

            @pl.when(jnp.logical_not(sides1[k].has))
            def _():
                pad[at1(mine)] = jnp.zeros(pad.at[at1(mine)].shape, pad.dtype)

            @pl.when(jnp.logical_not(sides2[k].has))
            def _():
                pad[at2(mine)] = jnp.zeros(pad.at[at2(mine)].shape, pad.dtype)

        for k in range(2):
            pl.when(sides1[1 - k].has)(copies1[k].wait_recv)
        copies2 = [
            remote(
                pad.at[at2(first if k == 0 else last)],
                pad.at[at2(high if k == 0 else low)],
                send.at[2 + k],
                recv.at[2 + k],
                sides2[k].where,
            )
            for k in range(2)
        ]
        for k in range(2):
            pl.when(sides2[k].has)(copies2[k].start)
        share1 = [
            remote(pad.at[at1(m)], pad.at[at1(m)], send.at[4 + k], recv.at[4 + k], partner)
            for k, m in enumerate((low, high))
        ]
        for c in share1:
            c.start()
        share2 = [
            remote(pad.at[at2(m)], pad.at[at2(m)], send.at[6 + k], recv.at[6 + k], partner)
            for k, m in enumerate((low, high))
        ]
        for k in range(2):
            pl.when(sides2[k].has)(copies2[1 - k].wait_recv)
            share2[k].start()
        for k in range(2):
            pl.when(sides1[k].has)(copies1[k].wait_send)
            pl.when(sides2[k].has)(copies2[k].wait_send)
        for c in share1 + share2:
            c.wait_send()

    def arriving(q, rows_first):
        def at1(piece):
            return (q, piece, own) if rows_first else (q, own, piece)

        def at2(piece):
            return (q, every, piece) if rows_first else (q, piece, every)

        for k, m in enumerate((low, high)):
            remote(pad.at[at1(m)], pad.at[at1(m)], send.at[4 + k], recv.at[4 + k], partner).wait_recv()
        for k, m in enumerate((low, high)):
            remote(pad.at[at2(m)], pad.at[at2(m)], send.at[6 + k], recv.at[6 + k], partner).wait_recv()

    @pl.when(p == 0)
    def _():
        role(0, (left, right), (up, down), False)
        arriving(1, True)

    @pl.when(p == 1)
    def _():
        role(1, (up, down), (left, right), True)
        arriving(0, False)


def dot(a, b):
    return jnp.dot(a, b, preferred_element_type=jnp.float32)


def step_kernel(offsets, pad, probe, amplitudes, table_a, table_b, grad, probe_grad):
    m = probe.shape[1]
    tall, span = m + 8, m + 128
    pr, pi = probe[0], probe[1]
    power = pr * pr + pi * pi
    grad[...] = jnp.zeros(grad.shape, grad.dtype)
    blank_rows = jnp.zeros((tall - m, m), jnp.float32)
    blank_cols = jnp.zeros((tall, span - m), jnp.float32)
    bf = jnp.bfloat16
    sum_r = sum_i = None
    for j in range(amplitudes.shape[0]):
        row, col = offsets[j, 0], offsets[j, 1]
        row_in, col_in = lax.rem(row, 8), lax.rem(col, 128)
        rows = pl.ds(pl.multiple_of(row - row_in, 8), tall)
        cols = pl.ds(pl.multiple_of(col - col_in, 128), span)

        def window(k):
            block = pad[k, rows, cols]
            block = pltpu.roll(block, lax.rem(span - col_in, span), 1)[:, :m]
            return pltpu.roll(block, lax.rem(tall - row_in, tall), 0)[:m]

        ar, ai = window(0), window(1)
        er = pr * ar - pi * ai
        ei = pr * ai + pi * ar
        half = dot(table_a[...], jnp.concatenate([er.astype(bf), ei.astype(bf)], 0)).astype(bf)
        far = dot(jnp.concatenate([half[:m], half[m:]], 1), table_b[...])
        fr, fi = far[:, :m], far[:, m:]
        ratio = amplitudes[j].astype(jnp.float32) / jnp.maximum(jnp.sqrt(fr * fr + fi * fi), 0.2)
        projected = jnp.concatenate([(fr * ratio).astype(bf), (fi * ratio).astype(bf)], 0)
        back_half = dot(table_b[...], projected).astype(bf)
        back = dot(jnp.concatenate([back_half[:m], back_half[m:]], 1), table_a[...])
        dr = back[:, :m] - er
        di = back[:, m:] - ei
        for k, term in enumerate((pr * dr + pi * di, pr * di - pi * dr, power)):
            moved = pltpu.roll(jnp.concatenate([term, blank_rows], 0), row_in, 0)
            moved = pltpu.roll(jnp.concatenate([moved, blank_cols], 1), col_in, 1)
            grad[k, rows, cols] = grad[k, rows, cols] + moved
        tr = ar * dr + ai * di
        ti = ar * di - ai * dr
        sum_r = tr if sum_r is None else sum_r + tr
        sum_i = ti if sum_i is None else sum_i + ti
    lanes = probe_grad.shape[2]
    for k, value in enumerate((sum_r, sum_i)):
        for h in range(m // lanes):
            probe_grad[k, h * m : (h + 1) * m, :] = value[:, h * lanes : (h + 1) * lanes]


def reduce_kernel(
    nx, ny, grad, prob, core, total, pair, acc, zr1, xr1, zr2, xr2, ppair, pacc, pr1, pr2, send, recv, psend, precv
):
    w = grad.shape[-1]
    q4 = w // 4
    p = lax.axis_index("pos")
    partner = {"pos": 1 - p}
    up, down = Side("scanx", nx, -1), Side("scanx", nx, 1)
    left, right = Side("scany", ny, -1), Side("scany", ny, 1)
    mx, my = lax.axis_index("scanx"), lax.axis_index("scany")
    greet(
        [(True, partner)]
        + [(True, {"scanx": lax.rem(mx + d, nx)}) for d in range(1, nx)]
        + [(True, {"scany": lax.rem(my + d, ny)}) for d in range(1, ny)]
    )

    def role(q, axis1, n1, axis2, n2, sides1, sides2, rows_first):
        o = 1 - q
        me1, me2 = lax.axis_index(axis1), lax.axis_index(axis2)
        c_prob = remote(prob.at[o], ppair, psend.at[0, 0], precv.at[0, 0], partner)
        c_prob.start()
        c_ch = remote(grad.at[o], pair.at[:, 0:2], send.at[0], recv.at[0], partner)
        c_ill = remote(grad.at[2, :, o], pair.at[:, 2], send.at[1], recv.at[1], partner)
        c_ch.start()
        c_ill.start()

        def scatter(stage, n, axis, me, src, size, landing):
            out = []
            for d in range(1, n):
                j = lax.rem(me + d, n)
                out.append(
                    remote(
                        src.at[pl.ds(j * size, size)],
                        landing.at[pl.ds(d * size, size)],
                        psend.at[stage, d],
                        precv.at[stage, d],
                        {axis: j},
                    )
                )
            for c in out:
                c.start()
            return out

        def gather(stage, n, axis, me, piece):
            out = []
            for d in range(1, n):
                out.append(
                    remote(
                        total.at[q, piece],
                        total.at[q, piece],
                        psend.at[stage, d],
                        precv.at[stage, d],
                        {axis: lax.rem(me + d, n)},
                    )
                )
            for c in out:
                c.start()
            return out

        c_prob.wait_recv()
        pacc[...] = prob[q] + ppair[...]
        c1 = scatter(1, n1, axis1, me1, pacc, n2, pr1)

        c_ch.wait_recv()
        c_ill.wait_recv()
        acc[:, 0:2] = grad[q] + pair[:, 0:2]
        acc[:, 2] = grad[2, :, q] + pair[:, 2]
        rim1 = zr1 if rows_first else xr1
        rim2 = xr2 if rows_first else zr2
        if rows_first:
            src1 = [acc.at[0], acc.at[3]]
            src2 = [acc.at[1:3, :, :, 0:q4], acc.at[1:3, :, :, 3 * q4 : w]]
        else:
            src1 = [acc.at[:, :, :, 0:q4], acc.at[:, :, :, 3 * q4 : w]]
            src2 = [acc.at[0, :, :, q4 : 3 * q4], acc.at[3, :, :, q4 : 3 * q4]]

        def fold(k, rim, rows, inner):
            if rows:
                g = 2 if k == 0 else 1
                cols = pl.ds(q4, 2 * q4) if inner else pl.ds(0, w)
                acc[g, :, :, cols] = acc[g, :, :, cols] + rim[k]
            else:
                cols = pl.ds(2 * q4, q4) if k == 0 else pl.ds(q4, q4)
                groups = pl.ds(1, 2) if inner else pl.ds(0, 4)
                acc[groups, :, :, cols] = acc[groups, :, :, cols] + rim[k]

        g1 = [remote(src1[k], rim1.at[k], send.at[2 + k], recv.at[2 + k], sides1[k].where) for k in range(2)]
        for k in range(2):
            pl.when(sides1[k].has)(g1[k].start)

        for c in c1:
            c.wait_recv()
        mine = pacc[pl.ds(me1 * n2, n2)]
        for d in range(1, n1):
            mine = mine + pr1[d * n2 : (d + 1) * n2]
        p1 = ppair
        p1[0:n2] = mine
        c2 = scatter(2, n2, axis2, me2, p1, 1, pr2)

        for k in range(2):

            @pl.when(sides1[1 - k].has)
            def _():
                g1[k].wait_recv()
                fold(k, rim1, rows_first, False)

        g2 = [remote(src2[k], rim2.at[k], send.at[4 + k], recv.at[4 + k], sides2[k].where) for k in range(2)]
        for k in range(2):
            pl.when(sides2[k].has)(g2[k].start)

        for c in c2:
            c.wait_recv()
        one = p1[pl.ds(me2, 1)]
        for d in range(1, n2):
            one = one + pr2[d : d + 1]
        total[q, pl.ds(me1 * n2 + me2, 1)] = one
        c3 = gather(3, n2, axis2, me2, pl.ds(me1 * n2 + me2, 1))

        for k in range(2):

            @pl.when(sides2[1 - k].has)
            def _():
                g2[k].wait_recv()
                fold(k, rim2, not rows_first, True)

        core[q] = acc[1:3, :, :, q4 : 3 * q4]
        c_core = remote(core.at[q], core.at[q], send.at[6], recv.at[6], partner)
        c_core.start()
        for c in c3:
            c.wait_recv()
        c4 = gather(4, n1, axis1, me1, pl.ds(me1 * n2, n2))
        for c in c4:
            c.wait_recv()
        c_tot = remote(total.at[q], total.at[q], psend.at[5, 0], precv.at[5, 0], partner)
        c_tot.start()
        for k in range(2):
            pl.when(sides1[k].has)(g1[k].wait_send)
            pl.when(sides2[k].has)(g2[k].wait_send)
        for c in [c_prob, c_ch, c_ill] + c1 + c2 + c3 + c4 + [c_core, c_tot]:
            c.wait_send()
        remote(core.at[o], core.at[o], send.at[6], recv.at[6], partner).wait_recv()
        remote(total.at[o], total.at[o], psend.at[5, 0], precv.at[5, 0], partner).wait_recv()

    @pl.when(p == 0)
    def _():
        role(0, "scany", ny, "scanx", nx, (left, right), (up, down), False)

    @pl.when(p == 1)
    def _():
        role(1, "scanx", nx, "scany", ny, (up, down), (left, right), True)


def tables(length):
    index = np.arange(length)
    angle = ((index[:, None] * index[None, :]) % length).astype(np.float32) * np.float32(2.0 * math.pi / length)
    scale = np.float32(1.0 / math.sqrt(length))
    c = np.cos(angle) * scale
    s = np.sin(angle) * scale
    a = np.block([[c, s], [-s, c]]).astype(jnp.bfloat16)
    b = np.block([[c, -s], [s, c]]).astype(jnp.bfloat16)
    return a, b


def shards(nx, ny, consts, specimen, probe_wave, amplitudes, offsets):
    m = probe_wave.shape[1]
    tile = specimen.shape[1]
    wide = tile + m
    f32 = jnp.float32
    vm = pl.BlockSpec(memory_space=VMEM)
    sm = pl.BlockSpec(memory_space=pltpu.SMEM)
    dma = pltpu.SemaphoreType.DMA
    pad = pl.pallas_call(
        functools.partial(halo_kernel, nx, ny),
        out_shape=jax.ShapeDtypeStruct((2, wide, wide), f32),
        in_specs=[vm],
        out_specs=vm,
        scratch_shapes=[dma((8,)), dma((8,))],
        compiler_params=pltpu.CompilerParams(collective_id=0, has_side_effects=True),
        name="halo",
    )(specimen)
    lanes = 128
    units = m * m // lanes
    grad, probe_grad = pl.pallas_call(
        step_kernel,
        out_shape=[
            jax.ShapeDtypeStruct((3, wide, wide), f32),
            jax.ShapeDtypeStruct((2, units, lanes), f32),
        ],
        in_specs=[sm] + [vm] * 5,
        out_specs=[vm, vm],
        name="step",
    )(offsets, pad, probe_wave, amplitudes, consts[0], consts[1])
    n = nx * ny
    s = units // n
    h = wide // 8
    most = max(nx, ny)
    core, total = pl.pallas_call(
        functools.partial(reduce_kernel, nx, ny),
        out_shape=[
            jax.ShapeDtypeStruct((2, 2, 3, h, wide // 2), f32),
            jax.ShapeDtypeStruct((2, n, s, lanes), f32),
        ],
        in_specs=[vm, vm],
        out_specs=[vm, vm],
        scratch_shapes=[
            VMEM((4, 3, h, wide), f32),
            VMEM((4, 3, h, wide), f32),
            VMEM((2, 3, h, wide), f32),
            VMEM((2, 4, 3, h, wide // 4), f32),
            VMEM((2, 3, h, wide // 2), f32),
            VMEM((2, 2, 3, h, wide // 4), f32),
            VMEM((n, s, lanes), f32),
            VMEM((n, s, lanes), f32),
            VMEM((n, s, lanes), f32),
            VMEM((most, s, lanes), f32),
            dma((7,)),
            dma((7,)),
            dma((6, most)),
            dma((6, most)),
        ],
        compiler_params=pltpu.CompilerParams(collective_id=1, has_side_effects=True),
        name="reduce",
    )(grad.reshape(3, 4, 2, h, wide), probe_grad.reshape(2, n, s, lanes))
    parts = core[:, :, 0:2].reshape(2, tile, tile)
    light = core[:, :, 2].transpose(1, 0, 2, 3).reshape(tile, tile)
    new_specimen = specimen + parts / (light[None] + 1.0)
    step_size = 1.0 / math.sqrt(offsets.shape[0] * n * 2)
    summed = total.reshape(2, m // lanes, m, lanes).transpose(0, 2, 1, 3).reshape(2, m, m)
    return new_specimen, probe_wave + summed * step_size


def solution(mesh):
    nx, ny = mesh.shape["scanx"], mesh.shape["scany"]

    def run(specimen, probe_wave, amplitudes, offsets):
        consts = tables(probe_wave.shape[2])
        return jax.shard_map(
            lambda *args: shards(nx, ny, [jnp.asarray(t) for t in consts], *args),
            mesh=mesh,
            in_specs=(
                P(None, ("groups", "scanx"), "scany"),
                P(None, "groups", None),
                P(("groups", "scanx", "scany", "pos"), None, None),
                P(("groups", "scanx", "scany", "pos"), None),
            ),
            out_specs=(P(None, ("groups", "scanx"), "scany"), P(None, "groups", None)),
            check_vma=False,
        )(specimen, probe_wave, amplitudes, offsets)

    return run
```

```python
import functools
import math

import jax
import jax.numpy as jnp
import numpy as np
from jax import lax
from jax.experimental import pallas as pl
from jax.experimental.pallas import tpu as pltpu
from jax.sharding import PartitionSpec as P

MESH = pl.DeviceIdType.MESH
VMEM = pltpu.VMEM


def remote(src, dst, send, recv, where):
    return pltpu.make_async_remote_copy(
        src_ref=src, dst_ref=dst, send_sem=send, recv_sem=recv, device_id=where, device_id_type=MESH
    )


def greet(conditions_devices):
    barrier = pltpu.get_barrier_semaphore()
    for present, where in conditions_devices:
        if present is True:
            pl.semaphore_signal(barrier, inc=1, device_id=where, device_id_type=MESH)
        else:

            @pl.when(present)
            def _(where=where):
                pl.semaphore_signal(barrier, inc=1, device_id=where, device_id_type=MESH)

    fixed = sum(1 for present, _ in conditions_devices if present is True)
    peers = [present.astype(jnp.int32) for present, _ in conditions_devices if present is not True]
    pl.semaphore_wait(barrier, sum(peers, fixed))


class Side:
    def __init__(self, axis, count, step):
        me = lax.axis_index(axis)
        self.has = me > 0 if step < 0 else me < count - 1
        self.where = {axis: me + step}


class Role:
    def __init__(self, q, nx, ny):
        along_x = ("scanx", nx, Side("scanx", nx, -1), Side("scanx", nx, 1))
        along_y = ("scany", ny, Side("scany", ny, -1), Side("scany", ny, 1))
        one, two = (along_y, along_x) if q == 0 else (along_x, along_y)
        self.q, self.o, self.rows_first = q, 1 - q, q == 1
        self.axis1, self.n1, self.sides1 = one[0], one[1], one[2:]
        self.axis2, self.n2, self.sides2 = two[0], two[1], two[2:]
        self.me1, self.me2 = lax.axis_index(self.axis1), lax.axis_index(self.axis2)


def when(*conditions):
    return pl.when(functools.reduce(jnp.logical_and, conditions))


def dot(a, b):
    return jnp.dot(a, b, preferred_element_type=jnp.float32)


class Halo:
    def __init__(self, role, spec, pad, send, recv, partner):
        self.r, self.spec, self.pad, self.partner = role, spec, pad, partner
        self.send, self.recv = send, recv
        tile = spec.shape[1]
        half = (pad.shape[1] - tile) // 2
        self.own = pl.ds(half, tile)
        self.margins = (pl.ds(0, half), pl.ds(half + tile, half))
        self.edges = (pl.ds(0, half), pl.ds(tile - half, half))
        self.pad_edges = (pl.ds(half, half), pl.ds(tile, half))
        self.whole = pl.ds(0, tile)

    def at(self, one, two):
        return (self.r.q, one, two) if self.r.rows_first else (self.r.q, two, one)

    def copy(self, src, dst, i, where):
        return remote(src, dst, self.send.at[i], self.recv.at[i], where)

    def strip1(self, m):
        return self.copy(
            self.spec.at[self.at(self.edges[1 - m], self.whole)],
            self.pad.at[self.at(self.margins[m], self.own)],
            m,
            self.r.sides1[1 - m].where,
        )

    def strip2(self, m):
        return self.copy(
            self.spec.at[self.at(self.whole, self.edges[1 - m])],
            self.pad.at[self.at(self.own, self.margins[m])],
            2 + m,
            self.r.sides2[1 - m].where,
        )

    def corner(self, m1, m2):
        return self.copy(
            self.pad.at[self.at(self.margins[m1], self.pad_edges[1 - m2])],
            self.pad.at[self.at(self.margins[m1], self.margins[m2])],
            4 + 2 * m1 + m2,
            self.r.sides2[1 - m2].where,
        )

    def share(self, i, one, two):
        ref = self.pad.at[self.at(one, two)]
        return self.copy(ref, ref, 8 + i, self.partner)

    def share1(self, m):
        return self.share(m, self.margins[m], self.own)

    def share2(self, m):
        return self.share(2 + m, self.own, self.margins[m])

    def share_corner(self, m1, m2):
        return self.share(4 + 2 * m1 + m2, self.margins[m1], self.margins[m2])

    def begin(self):
        for m in range(2):
            when(self.r.sides1[1 - m].has)(self.strip1(m).start)
        for m in range(2):
            when(self.r.sides2[1 - m].has)(self.strip2(m).start)

    def relay(self):
        r = self.r
        for m1 in range(2):

            @when(r.sides1[m1].has)
            def _():
                self.strip1(m1).wait_recv()
                for m2 in range(2):
                    when(r.sides2[1 - m2].has)(self.corner(m1, m2).start)
                self.share1(m1).start()

        for m in range(2):

            @when(r.sides2[m].has)
            def _():
                self.strip2(m).wait_recv()
                self.share2(m).start()

        for m1 in range(2):
            for m2 in range(2):

                @when(r.sides1[m1].has, r.sides2[m2].has)
                def _():
                    self.corner(m1, m2).wait_recv()
                    self.share_corner(m1, m2).start()

    def arrive(self):
        r = self.r
        for m in range(2):
            when(r.sides1[m].has)(self.share1(m).wait_recv)
            when(r.sides2[m].has)(self.share2(m).wait_recv)
        for m1 in range(2):
            for m2 in range(2):
                when(r.sides1[m1].has, r.sides2[m2].has)(self.share_corner(m1, m2).wait_recv)

    def finish(self):
        r = self.r
        for m in range(2):
            when(r.sides1[1 - m].has)(self.strip1(m).wait_send)
            when(r.sides2[1 - m].has)(self.strip2(m).wait_send)
            when(r.sides1[m].has)(self.share1(m).wait_send)
            when(r.sides2[m].has)(self.share2(m).wait_send)
        for m1 in range(2):
            for m2 in range(2):
                when(r.sides1[m1].has, r.sides2[1 - m2].has)(self.corner(m1, m2).wait_send)
                when(r.sides1[m1].has, r.sides2[m2].has)(self.share_corner(m1, m2).wait_send)


class Fold:
    def __init__(self, role, mine, theirs, pair, acc, rims, core, send, recv, partner):
        self.r, self.mine, self.theirs, self.pair, self.acc = role, mine, theirs, pair, acc
        self.xr1, self.xr2, self.zr1, self.zr2 = rims
        self.core, self.send, self.recv, self.partner = core, send, recv, partner
        w = acc.shape[-1]
        self.w, self.q4 = w, w // 4

    def pieces(self, rows):
        q4, w = self.q4, self.w
        if rows:
            return [(pl.ds(0, 1),), (pl.ds(3, 1),), (pl.ds(1, 2),)]
        lead = (slice(None),) * 3
        return [lead + (pl.ds(0, q4),), lead + (pl.ds(3 * q4, q4),), lead + (pl.ds(q4, 2 * q4),)]

    def pair_copy(self, i, rows):
        at = self.pieces(rows)[i]
        return remote(self.theirs.at[at], self.pair.at[at], self.send.at[i], self.recv.at[i], self.partner)

    def begin(self):
        for i in range(3):
            self.pair_copy(i, not self.r.rows_first).start()

    def add(self, i):
        self.pair_copy(i, self.r.rows_first).wait_recv()
        at = self.pieces(self.r.rows_first)[i]
        self.acc[at] = self.mine[at] + self.pair[at]

    def rim_copy(self, stage, m):
        r, q4, w = self.r, self.q4, self.w
        rows = r.rows_first == (stage == 0)
        k = 1 - m
        if rows:
            cols = pl.ds(0, w) if stage == 0 else pl.ds(q4, 2 * q4)
            src = self.acc.at[3 * k, :, :, cols]
            rim = self.zr1 if stage == 0 else self.zr2
        else:
            groups = pl.ds(0, 4) if stage == 0 else pl.ds(1, 2)
            src = self.acc.at[groups, :, :, pl.ds(3 * k * q4, q4)]
            rim = self.xr1 if stage == 0 else self.xr2
        sides = r.sides1 if stage == 0 else r.sides2
        i = 3 + 2 * stage + m
        return remote(src, rim.at[m], self.send.at[i], self.recv.at[i], sides[k].where)

    def send_rims(self, stage):
        sides = self.r.sides1 if stage == 0 else self.r.sides2
        for m in range(2):
            when(sides[1 - m].has)(self.rim_copy(stage, m).start)

    def fold(self, stage):
        r, q4, w, acc = self.r, self.q4, self.w, self.acc
        rows = r.rows_first == (stage == 0)
        sides = r.sides1 if stage == 0 else r.sides2
        for m in range(2):

            @when(sides[m].has)
            def _():
                self.rim_copy(stage, m).wait_recv()
                if rows:
                    cols = pl.ds(0, w) if stage == 0 else pl.ds(q4, 2 * q4)
                    rim = self.zr1 if stage == 0 else self.zr2
                    acc[1 + m, :, :, cols] = acc[1 + m, :, :, cols] + rim[m]
                else:
                    groups = pl.ds(0, 4) if stage == 0 else pl.ds(1, 2)
                    cols = pl.ds((1 + m) * q4, q4)
                    rim = self.xr1 if stage == 0 else self.xr2
                    acc[groups, :, :, cols] = acc[groups, :, :, cols] + rim[m]

    def share_copy(self, q):
        return remote(self.core.at[q], self.core.at[q], self.send.at[7], self.recv.at[7], self.partner)

    def share(self):
        q4 = self.q4
        self.core[self.r.q] = self.acc[1:3, :, :, q4 : 3 * q4]
        self.share_copy(self.r.q).start()

    def arrive(self):
        self.share_copy(self.r.o).wait_recv()

    def finish(self):
        r = self.r
        for i in range(3):
            self.pair_copy(i, not r.rows_first).wait_send()
        for m in range(2):
            when(r.sides1[1 - m].has)(self.rim_copy(0, m).wait_send)
            when(r.sides2[1 - m].has)(self.rim_copy(1, m).wait_send)
        self.share_copy(r.q).wait_send()


class ProbeSum:
    def __init__(self, role, mine, theirs, ppair, pacc, p1, pr1, pr2, total, send, recv, partner):
        self.r, self.mine, self.theirs = role, mine, theirs
        self.ppair, self.pacc, self.p1 = ppair, pacc, p1
        self.pr1, self.pr2, self.total = pr1, pr2, total
        self.send, self.recv, self.partner = send, recv, partner

    def copy(self, src, dst, stage, d, where):
        return remote(src, dst, self.send.at[stage, d], self.recv.at[stage, d], where)

    def pair_copy(self):
        return self.copy(self.theirs, self.ppair, 0, 0, self.partner)

    def begin(self):
        self.pair_copy().start()

    def scatter1(self):
        r = self.r
        out = []
        for d in range(1, r.n1):
            j = lax.rem(r.me1 + d, r.n1)
            src = self.pacc.at[pl.ds(j * r.n2, r.n2)]
            out.append(self.copy(src, self.pr1.at[pl.ds(d * r.n2, r.n2)], 1, d, {r.axis1: j}))
        return out

    def scatter2(self):
        r = self.r
        out = []
        for d in range(1, r.n2):
            j = lax.rem(r.me2 + d, r.n2)
            out.append(self.copy(self.p1.at[pl.ds(j, 1)], self.pr2.at[pl.ds(d, 1)], 2, d, {r.axis2: j}))
        return out

    def gather2(self, back):
        r = self.r
        out = []
        for d in range(1, r.n2):
            j = lax.rem(r.me2 + d, r.n2)
            origin = lax.rem(r.me2 - d + r.n2, r.n2) if back else r.me2
            ref = self.total.at[r.q, pl.ds(r.me1 * r.n2 + origin, 1)]
            out.append(self.copy(ref, ref, 3, d, {r.axis2: j}))
        return out

    def gather1(self, back):
        r = self.r
        out = []
        for d in range(1, r.n1):
            j = lax.rem(r.me1 + d, r.n1)
            origin = lax.rem(r.me1 - d + r.n1, r.n1) if back else r.me1
            ref = self.total.at[r.q, pl.ds(origin * r.n2, r.n2)]
            out.append(self.copy(ref, ref, 4, d, {r.axis1: j}))
        return out

    def share_copy(self, d, sender):
        r = self.r
        origin = lax.rem(r.me1 - d + r.n1, r.n1)
        ref = self.total.at[r.q, pl.ds(origin * r.n2, r.n2)]
        return self.copy(ref, ref, 5, d, self.partner)

    def step1(self):
        self.pair_copy().wait_recv()
        self.pacc[...] = self.mine[...] + self.ppair[...]
        for c in self.scatter1():
            c.start()

    def step2(self):
        r = self.r
        mine = self.pacc[pl.ds(r.me1 * r.n2, r.n2)]
        for d, c in enumerate(self.scatter1(), 1):
            c.wait_recv()
            mine = mine + self.pr1[d * r.n2 : (d + 1) * r.n2]
        self.p1[0 : r.n2] = mine
        for c in self.scatter2():
            c.start()

    def step3(self):
        r = self.r
        one = self.p1[pl.ds(r.me2, 1)]
        for d, c in enumerate(self.scatter2(), 1):
            c.wait_recv()
            one = one + self.pr2[d : d + 1]
        self.total[r.q, pl.ds(r.me1 * r.n2 + r.me2, 1)] = one
        for c in self.gather2(0):
            c.start()

    def step4(self):
        for c in self.gather2(1):
            c.wait_recv()
        for c in self.gather1(0):
            c.start()
        self.share_copy(0, True).start()

    def step5(self):
        for d, c in enumerate(self.gather1(1), 1):
            c.wait_recv()
            self.share_copy(d, True).start()

    def arrive(self):
        for d in range(self.r.n1):
            self.share_copy(d, False).wait_recv()

    def finish(self):
        self.pair_copy().wait_send()
        for c in self.scatter1() + self.scatter2() + self.gather2(0) + self.gather1(0):
            c.wait_send()
        for d in range(self.r.n1):
            self.share_copy(d, True).wait_send()


def line_greet(nx, ny, partner):
    mx, my = lax.axis_index("scanx"), lax.axis_index("scany")
    greet(
        [(True, partner)]
        + [(True, {"scanx": lax.rem(mx + d, nx)}) for d in range(1, nx)]
        + [(True, {"scany": lax.rem(my + d, ny)}) for d in range(1, ny)]
    )


def each(step):
    p = lax.axis_index("pos")
    for q in range(2):
        pl.when(p == q)(functools.partial(step, q))


def halo_kernel(nx, ny, spec, pad, send, recv, local):
    tile = spec.shape[1]
    half = (pad.shape[1] - tile) // 2
    own = pl.ds(half, tile)
    partner = {"pos": 1 - lax.axis_index("pos")}
    centre = pltpu.make_async_copy(spec, pad.at[:, own, own], local.at[0])
    centre.start()
    roles = [Role(q, nx, ny) for q in range(2)]
    sides = roles[1].sides1 + roles[0].sides1
    greet([(True, partner)] + [(side.has, side.where) for side in sides])
    halos = [Halo(r, spec, pad, send, recv, partner) for r in roles]
    each(lambda q: halos[q].begin())
    for i, at in enumerate(
        (
            (slice(None), pl.ds(0, half)),
            (slice(None), pl.ds(half + tile, half)),
            (slice(None), slice(None), pl.ds(0, half)),
            (slice(None), slice(None), pl.ds(half + tile, half)),
        )
    ):

        @pl.when(jnp.logical_not(sides[i].has))
        def _(at=at):
            pad[at] = jnp.zeros(pad.at[at].shape, pad.dtype)

    def rest(q):
        halos[q].relay()
        halos[1 - q].arrive()
        halos[q].finish()

    each(rest)
    centre.wait()


def step_kernel(offsets, pad, probe, amplitudes, table_a, table_b, grad_out, prob, grad, local):
    m = probe.shape[1]
    tall, span = m + 8, m + 128
    pr, pi = probe[0], probe[1]
    grad[...] = jnp.zeros(grad.shape, grad.dtype)
    blank_rows = jnp.zeros((tall - m, m), jnp.float32)
    blank_cols = jnp.zeros((tall, span - m), jnp.float32)
    bf = jnp.bfloat16
    positions = amplitudes.shape[0]

    def place_at(j):
        row, col = offsets[j, 0], offsets[j, 1]
        row_in, col_in = lax.rem(row, 8), lax.rem(col, 128)
        rows = pl.ds(pl.multiple_of(row - row_in, 8), tall)
        cols = pl.ds(pl.multiple_of(col - col_in, 128), span)
        return row_in, col_in, rows, cols

    def place(j, k, term):
        row_in, col_in, rows, cols = place_at(j)
        moved = pltpu.roll(jnp.concatenate([term, blank_rows], 0), row_in, 0)
        moved = pltpu.roll(jnp.concatenate([moved, blank_cols], 1), col_in, 1)
        grad[k, rows, cols] = grad[k, rows, cols] + moved

    outs = [pltpu.make_async_copy(grad.at[k], grad_out.at[k], local.at[k]) for k in range(3)]
    power = pr * pr + pi * pi
    for j in range(positions):
        place(j, 2, power)
    outs[2].start()
    sum_r = sum_i = None
    for j in range(positions):
        row_in, col_in, rows, cols = place_at(j)

        def window(k):
            block = pad[k, rows, cols]
            block = pltpu.roll(block, lax.rem(span - col_in, span), 1)[:, :m]
            return pltpu.roll(block, lax.rem(tall - row_in, tall), 0)[:m]

        ar, ai = window(0), window(1)
        er = pr * ar - pi * ai
        ei = pr * ai + pi * ar
        left = dot(table_a[...], jnp.concatenate([er.astype(bf), ei.astype(bf)], 0)).astype(bf)
        far = dot(jnp.concatenate([left[:m], left[m:]], 1), table_b[...])
        fr, fi = far[:, :m], far[:, m:]
        ratio = amplitudes[j].astype(jnp.float32) / jnp.maximum(jnp.sqrt(fr * fr + fi * fi), 0.2)
        projected = jnp.concatenate([(fr * ratio).astype(bf), (fi * ratio).astype(bf)], 0)
        back_half = dot(table_b[...], projected).astype(bf)
        back = dot(jnp.concatenate([back_half[:m], back_half[m:]], 1), table_a[...])
        dr = back[:, :m] - er
        di = back[:, m:] - ei
        tr = ar * dr + ai * di
        ti = ar * di - ai * dr
        sum_r = tr if sum_r is None else sum_r + tr
        sum_i = ti if sum_i is None else sum_i + ti
        place(j, 0, pr * dr + pi * di)
        if j == positions - 1:
            outs[0].start()
        place(j, 1, pr * di - pi * dr)
    outs[1].start()
    n, s, lanes = prob.shape[1:]
    for k, value in enumerate((sum_r, sum_i)):
        for c in range(n):
            r0, l0 = c * s % m, c * s // m * lanes
            prob[k, c] = value[r0 : r0 + s, l0 : l0 + lanes]
    for c in outs:
        c.wait()


def reduce_kernel(nx, ny, step_size, *refs):
    grad, prob, spec_in, probe_in, new_spec, new_probe = refs[:6]
    spec, probe, mine, imine, pmine, total = refs[6:12]
    (pair, acc, xr1, xr2, zr1, zr2, core, ipair, iacc, ixr1, ixr2, izr1, izr2, icore) = refs[12:26]
    (ppair, pacc, p1, pr1, pr2) = refs[26:31]
    (gsend, grecv, isend, irecv, psend, precv, local) = refs[31:]
    m = probe.shape[1]
    h = acc.shape[2]
    p = lax.axis_index("pos")
    partner = {"pos": 1 - p}
    loads = [
        pltpu.make_async_copy(src, dst, local.at[i])
        for i, (src, dst) in enumerate(
            (
                (prob.at[p], pmine),
                (grad.at[p], mine),
                (grad.at[2, :, pl.ds(p, 1)], imine),
                (spec_in, spec),
                (probe_in, probe),
            )
        )
    ]
    for c in loads:
        c.start()
    line_greet(nx, ny, partner)
    roles = [Role(q, nx, ny) for q in range(2)]
    folds = [
        Fold(r, mine, grad.at[r.o], pair, acc, (xr1, xr2, zr1, zr2), core, gsend, grecv, partner)
        for r in roles
    ]
    lights = [
        Fold(
            r,
            imine,
            grad.at[2, :, pl.ds(r.o, 1)],
            ipair,
            iacc,
            (ixr1, ixr2, izr1, izr2),
            icore,
            isend,
            irecv,
            partner,
        )
        for r in roles
    ]
    probes = [
        ProbeSum(r, pmine, prob.at[r.o], ppair, pacc, p1, pr1, pr2, total, psend, precv, partner)
        for r in roles
    ]

    def objects(q):
        probe_sum, fold, light = probes[q], folds[q], lights[q]
        probe_sum.begin()
        fold.begin()
        light.begin()
        loads[0].wait()
        probe_sum.step1()
        loads[1].wait()
        fold.add(0)
        fold.add(1)
        fold.send_rims(0)
        loads[2].wait()
        light.add(0)
        light.add(1)
        light.send_rims(0)
        fold.add(2)
        light.add(2)
        probe_sum.step2()
        fold.fold(0)
        fold.send_rims(1)
        light.fold(0)
        light.send_rims(1)
        probe_sum.step3()
        fold.fold(1)
        fold.share()
        light.fold(1)
        light.share()
        probe_sum.step4()
        light.arrive()
        fold.arrive()

    each(objects)
    loads[3].wait()
    for k in range(2):
        for g in range(2):
            for b in range(2):
                rows = slice((2 * g + b) * h, (2 * g + b + 1) * h)
                new_spec[k, rows] = spec[k, rows] + core[k, g, b] / (icore[b, g, 0] + 1.0)

    def closing(q):
        probes[q].step5()
        probes[1 - q].arrive()
        lights[q].finish()
        folds[q].finish()
        probes[q].finish()

    each(closing)
    loads[4].wait()
    n, s, lanes = prob.shape[1:]
    for k in range(2):
        for c in range(n):
            rows = slice(c * s % m, c * s % m + s)
            cols = slice(c * s // m * lanes, c * s // m * lanes + lanes)
            new_probe[k, rows, cols] = probe[k, rows, cols] + total[k, c] * step_size


def tables(length):
    index = np.arange(length)
    angle = ((index[:, None] * index[None, :]) % length).astype(np.float32) * np.float32(2.0 * math.pi / length)
    scale = np.float32(1.0 / math.sqrt(length))
    c = np.cos(angle) * scale
    s = np.sin(angle) * scale
    a = np.block([[c, s], [-s, c]]).astype(jnp.bfloat16)
    b = np.block([[c, -s], [s, c]]).astype(jnp.bfloat16)
    return a, b


def shards(nx, ny, consts, specimen, probe_wave, amplitudes, offsets):
    m = probe_wave.shape[1]
    tile = specimen.shape[1]
    wide = tile + m
    f32 = jnp.float32
    vm = pl.BlockSpec(memory_space=VMEM)
    sm = pl.BlockSpec(memory_space=pltpu.SMEM)
    anywhere = pl.BlockSpec(memory_space=pl.ANY)
    dma = pltpu.SemaphoreType.DMA
    lanes = 128
    n = nx * ny
    s = m * m // lanes // n
    h = wide // 8
    most = max(nx, ny)
    positions = offsets.shape[0]
    pad = pl.pallas_call(
        functools.partial(halo_kernel, nx, ny),
        out_shape=jax.ShapeDtypeStruct((2, wide, wide), f32),
        in_specs=[anywhere],
        out_specs=vm,
        scratch_shapes=[dma((16,)), dma((16,)), dma((1,))],
        compiler_params=pltpu.CompilerParams(collective_id=0, has_side_effects=True),
        name="halo",
    )(specimen)
    grad, prob = pl.pallas_call(
        step_kernel,
        out_shape=[
            jax.ShapeDtypeStruct((3, wide, wide), f32),
            jax.ShapeDtypeStruct((2, n, s, lanes), f32),
        ],
        in_specs=[sm] + [vm] * 5,
        out_specs=[anywhere, vm],
        scratch_shapes=[VMEM((3, wide, wide), f32), dma((3,))],
        name="step",
    )(offsets, pad, probe_wave, amplitudes, consts[0], consts[1])

    def field(size):
        return [
            VMEM((4, size, h, wide), f32),
            VMEM((4, size, h, wide), f32),
            VMEM((2, 4, size, h, wide // 4), f32),
            VMEM((2, 2, size, h, wide // 4), f32),
            VMEM((2, size, h, wide), f32),
            VMEM((2, size, h, wide // 2), f32),
            VMEM((2, 2, size, h, wide // 2), f32),
        ]

    step_size = 1.0 / math.sqrt(positions * n * 2)
    return pl.pallas_call(
        functools.partial(reduce_kernel, nx, ny, step_size),
        out_shape=[
            jax.ShapeDtypeStruct(specimen.shape, f32),
            jax.ShapeDtypeStruct(probe_wave.shape, f32),
        ],
        in_specs=[anywhere] * 4,
        out_specs=[vm, vm],
        scratch_shapes=[
            VMEM(specimen.shape, f32),
            VMEM(probe_wave.shape, f32),
            VMEM((4, 2, h, wide), f32),
            VMEM((4, 1, h, wide), f32),
            VMEM((n, s, lanes), f32),
            VMEM((2, n, s, lanes), f32),
            *field(2),
            *field(1),
            VMEM((n, s, lanes), f32),
            VMEM((n, s, lanes), f32),
            VMEM((most, s, lanes), f32),
            VMEM((n, s, lanes), f32),
            VMEM((most, s, lanes), f32),
            dma((8,)),
            dma((8,)),
            dma((8,)),
            dma((8,)),
            dma((6, most)),
            dma((6, most)),
            dma((5,)),
        ],
        compiler_params=pltpu.CompilerParams(collective_id=1, has_side_effects=True),
        name="reduce",
    )(grad.reshape(3, 4, 2, h, wide), prob, specimen, probe_wave)


def solution(mesh):
    nx, ny = mesh.shape["scanx"], mesh.shape["scany"]

    def run(specimen, probe_wave, amplitudes, offsets):
        consts = tables(probe_wave.shape[2])
        return jax.shard_map(
            lambda *args: shards(nx, ny, [jnp.asarray(t) for t in consts], *args),
            mesh=mesh,
            in_specs=(
                P(None, ("groups", "scanx"), "scany"),
                P(None, "groups", None),
                P(("groups", "scanx", "scany", "pos"), None, None),
                P(("groups", "scanx", "scany", "pos"), None),
            ),
            out_specs=(P(None, ("groups", "scanx"), "scany"), P(None, "groups", None)),
            check_vma=False,
        )(specimen, probe_wave, amplitudes, offsets)

    return run
```

```python
import functools
import math

import jax
import jax.numpy as jnp
import numpy as np
from jax import lax
from jax.experimental import pallas as pl
from jax.experimental.pallas import tpu as pltpu
from jax.sharding import PartitionSpec as P

MESH = pl.DeviceIdType.MESH
VMEM = pltpu.VMEM


def remote(src, dst, send, recv, where):
    return pltpu.make_async_remote_copy(
        src_ref=src, dst_ref=dst, send_sem=send, recv_sem=recv, device_id=where, device_id_type=MESH
    )


def greet(conditions_devices):
    barrier = pltpu.get_barrier_semaphore()
    for present, where in conditions_devices:
        if present is True:
            pl.semaphore_signal(barrier, inc=1, device_id=where, device_id_type=MESH)
        else:

            @pl.when(present)
            def _(where=where):
                pl.semaphore_signal(barrier, inc=1, device_id=where, device_id_type=MESH)

    fixed = sum(1 for present, _ in conditions_devices if present is True)
    peers = [present.astype(jnp.int32) for present, _ in conditions_devices if present is not True]
    pl.semaphore_wait(barrier, sum(peers, fixed))


class Side:
    def __init__(self, axis, count, step):
        me = lax.axis_index(axis)
        self.has = me > 0 if step < 0 else me < count - 1
        self.where = {axis: me + step}


class Role:
    def __init__(self, q, nx, ny):
        along_x = ("scanx", nx, Side("scanx", nx, -1), Side("scanx", nx, 1))
        along_y = ("scany", ny, Side("scany", ny, -1), Side("scany", ny, 1))
        one, two = (along_y, along_x) if q == 0 else (along_x, along_y)
        self.q, self.o, self.rows_first = q, 1 - q, q == 1
        self.axis1, self.n1, self.sides1 = one[0], one[1], one[2:]
        self.axis2, self.n2, self.sides2 = two[0], two[1], two[2:]
        self.me1, self.me2 = lax.axis_index(self.axis1), lax.axis_index(self.axis2)


def when(*conditions):
    return pl.when(functools.reduce(jnp.logical_and, conditions))


def dot(a, b):
    return jnp.dot(a, b, preferred_element_type=jnp.float32)


class Halo:
    def __init__(self, role, spec, pad, send, recv, partner):
        self.r, self.spec, self.pad, self.partner = role, spec, pad, partner
        self.send, self.recv = send, recv
        tile = spec.shape[1]
        half = (pad.shape[1] - tile) // 2
        self.own = pl.ds(half, tile)
        self.margins = (pl.ds(0, half), pl.ds(half + tile, half))
        self.edges = (pl.ds(0, half), pl.ds(tile - half, half))
        self.pad_edges = (pl.ds(half, half), pl.ds(tile, half))
        self.whole = pl.ds(0, tile)

    def at(self, one, two):
        return (self.r.q, one, two) if self.r.rows_first else (self.r.q, two, one)

    def copy(self, src, dst, i, where):
        return remote(src, dst, self.send.at[i], self.recv.at[i], where)

    def strip1(self, m):
        return self.copy(
            self.spec.at[self.at(self.edges[1 - m], self.whole)],
            self.pad.at[self.at(self.margins[m], self.own)],
            m,
            self.r.sides1[1 - m].where,
        )

    def strip2(self, m):
        return self.copy(
            self.spec.at[self.at(self.whole, self.edges[1 - m])],
            self.pad.at[self.at(self.own, self.margins[m])],
            2 + m,
            self.r.sides2[1 - m].where,
        )

    def corner(self, m1, m2):
        return self.copy(
            self.pad.at[self.at(self.margins[m1], self.pad_edges[1 - m2])],
            self.pad.at[self.at(self.margins[m1], self.margins[m2])],
            4 + 2 * m1 + m2,
            self.r.sides2[1 - m2].where,
        )

    def share(self, i, one, two):
        ref = self.pad.at[self.at(one, two)]
        return self.copy(ref, ref, 8 + i, self.partner)

    def share1(self, m):
        return self.share(m, self.margins[m], self.own)

    def share2(self, m):
        return self.share(2 + m, self.own, self.margins[m])

    def share_corner(self, m1, m2):
        return self.share(4 + 2 * m1 + m2, self.margins[m1], self.margins[m2])

    def begin(self):
        for m in range(2):
            when(self.r.sides1[1 - m].has)(self.strip1(m).start)
        for m in range(2):
            when(self.r.sides2[1 - m].has)(self.strip2(m).start)

    def relay(self):
        r = self.r
        for m1 in range(2):

            @when(r.sides1[m1].has)
            def _():
                self.strip1(m1).wait_recv()
                for m2 in range(2):
                    when(r.sides2[1 - m2].has)(self.corner(m1, m2).start)
                self.share1(m1).start()

        for m in range(2):

            @when(r.sides2[m].has)
            def _():
                self.strip2(m).wait_recv()
                self.share2(m).start()

        for m1 in range(2):
            for m2 in range(2):

                @when(r.sides1[m1].has, r.sides2[m2].has)
                def _():
                    self.corner(m1, m2).wait_recv()
                    self.share_corner(m1, m2).start()

    def arrive(self):
        r = self.r
        for m in range(2):
            when(r.sides1[m].has)(self.share1(m).wait_recv)
            when(r.sides2[m].has)(self.share2(m).wait_recv)
        for m1 in range(2):
            for m2 in range(2):
                when(r.sides1[m1].has, r.sides2[m2].has)(self.share_corner(m1, m2).wait_recv)

    def finish(self):
        r = self.r
        for m in range(2):
            when(r.sides1[1 - m].has)(self.strip1(m).wait_send)
            when(r.sides2[1 - m].has)(self.strip2(m).wait_send)
            when(r.sides1[m].has)(self.share1(m).wait_send)
            when(r.sides2[m].has)(self.share2(m).wait_send)
        for m1 in range(2):
            for m2 in range(2):
                when(r.sides1[m1].has, r.sides2[1 - m2].has)(self.corner(m1, m2).wait_send)
                when(r.sides1[m1].has, r.sides2[m2].has)(self.share_corner(m1, m2).wait_send)


class Fold:
    def __init__(self, role, mine, theirs, pair, acc, rims, core, send, recv, partner):
        self.r, self.mine, self.theirs, self.pair, self.acc = role, mine, theirs, pair, acc
        self.xr1, self.xr2, self.zr1, self.zr2 = rims
        self.core, self.send, self.recv, self.partner = core, send, recv, partner
        w = acc.shape[-1]
        self.w, self.q4 = w, w // 4

    def pieces(self, rows):
        q4, w = self.q4, self.w
        if rows:
            return [(pl.ds(0, 1),), (pl.ds(3, 1),), (pl.ds(1, 2),)]
        lead = (slice(None),) * 3
        return [lead + (pl.ds(0, q4),), lead + (pl.ds(3 * q4, q4),), lead + (pl.ds(q4, 2 * q4),)]

    def pair_copy(self, i, rows):
        at = self.pieces(rows)[i]
        return remote(self.theirs.at[at], self.pair.at[at], self.send.at[i], self.recv.at[i], self.partner)

    def begin(self):
        for i in range(3):
            self.pair_copy(i, not self.r.rows_first).start()

    def add(self, i):
        self.pair_copy(i, self.r.rows_first).wait_recv()
        at = self.pieces(self.r.rows_first)[i]
        self.acc[at] = self.mine[at] + self.pair[at]

    def rim_copy(self, stage, m):
        r, q4, w = self.r, self.q4, self.w
        rows = r.rows_first == (stage == 0)
        k = 1 - m
        if rows:
            cols = pl.ds(0, w) if stage == 0 else pl.ds(q4, 2 * q4)
            src = self.acc.at[3 * k, :, :, cols]
            rim = self.zr1 if stage == 0 else self.zr2
        else:
            groups = pl.ds(0, 4) if stage == 0 else pl.ds(1, 2)
            src = self.acc.at[groups, :, :, pl.ds(3 * k * q4, q4)]
            rim = self.xr1 if stage == 0 else self.xr2
        sides = r.sides1 if stage == 0 else r.sides2
        i = 3 + 2 * stage + m
        return remote(src, rim.at[m], self.send.at[i], self.recv.at[i], sides[k].where)

    def send_rims(self, stage):
        sides = self.r.sides1 if stage == 0 else self.r.sides2
        for m in range(2):
            when(sides[1 - m].has)(self.rim_copy(stage, m).start)

    def fold(self, stage):
        r, q4, w, acc = self.r, self.q4, self.w, self.acc
        rows = r.rows_first == (stage == 0)
        sides = r.sides1 if stage == 0 else r.sides2
        for m in range(2):

            @when(sides[m].has)
            def _():
                self.rim_copy(stage, m).wait_recv()
                if rows:
                    cols = pl.ds(0, w) if stage == 0 else pl.ds(q4, 2 * q4)
                    rim = self.zr1 if stage == 0 else self.zr2
                    acc[1 + m, :, :, cols] = acc[1 + m, :, :, cols] + rim[m]
                else:
                    groups = pl.ds(0, 4) if stage == 0 else pl.ds(1, 2)
                    cols = pl.ds((1 + m) * q4, q4)
                    rim = self.xr1 if stage == 0 else self.xr2
                    acc[groups, :, :, cols] = acc[groups, :, :, cols] + rim[m]

    def share_copy(self, q):
        return remote(self.core.at[q], self.core.at[q], self.send.at[7], self.recv.at[7], self.partner)

    def share(self):
        q4 = self.q4
        self.core[self.r.q] = self.acc[1:3, :, :, q4 : 3 * q4]
        self.share_copy(self.r.q).start()

    def arrive(self):
        self.share_copy(self.r.o).wait_recv()

    def finish(self):
        r = self.r
        for i in range(3):
            self.pair_copy(i, not r.rows_first).wait_send()
        for m in range(2):
            when(r.sides1[1 - m].has)(self.rim_copy(0, m).wait_send)
            when(r.sides2[1 - m].has)(self.rim_copy(1, m).wait_send)
        self.share_copy(r.q).wait_send()


class ProbeSum:
    def __init__(self, role, mine, theirs, ppair, pacc, p1, pr1, pr2, total, send, recv, partner):
        self.r, self.mine, self.theirs = role, mine, theirs
        self.ppair, self.pacc, self.p1 = ppair, pacc, p1
        self.pr1, self.pr2, self.total = pr1, pr2, total
        self.send, self.recv, self.partner = send, recv, partner

    def copy(self, src, dst, stage, d, where):
        return remote(src, dst, self.send.at[stage, d], self.recv.at[stage, d], where)

    def pair_copy(self):
        return self.copy(self.theirs, self.ppair, 0, 0, self.partner)

    def begin(self):
        self.pair_copy().start()

    def scatter1(self):
        r = self.r
        out = []
        for d in range(1, r.n1):
            j = lax.rem(r.me1 + d, r.n1)
            src = self.pacc.at[pl.ds(j * r.n2, r.n2)]
            out.append(self.copy(src, self.pr1.at[pl.ds(d * r.n2, r.n2)], 1, d, {r.axis1: j}))
        return out

    def scatter2(self):
        r = self.r
        out = []
        for d in range(1, r.n2):
            j = lax.rem(r.me2 + d, r.n2)
            out.append(self.copy(self.p1.at[pl.ds(j, 1)], self.pr2.at[pl.ds(d, 1)], 2, d, {r.axis2: j}))
        return out

    def gather2(self, back):
        r = self.r
        out = []
        for d in range(1, r.n2):
            j = lax.rem(r.me2 + d, r.n2)
            origin = lax.rem(r.me2 - d + r.n2, r.n2) if back else r.me2
            ref = self.total.at[r.q, pl.ds(r.me1 * r.n2 + origin, 1)]
            out.append(self.copy(ref, ref, 3, d, {r.axis2: j}))
        return out

    def gather1(self, back):
        r = self.r
        out = []
        for d in range(1, r.n1):
            j = lax.rem(r.me1 + d, r.n1)
            origin = lax.rem(r.me1 - d + r.n1, r.n1) if back else r.me1
            ref = self.total.at[r.q, pl.ds(origin * r.n2, r.n2)]
            out.append(self.copy(ref, ref, 4, d, {r.axis1: j}))
        return out

    def share_copy(self, d, sender):
        r = self.r
        origin = lax.rem(r.me1 - d + r.n1, r.n1)
        ref = self.total.at[r.q, pl.ds(origin * r.n2, r.n2)]
        return self.copy(ref, ref, 5, d, self.partner)

    def step1(self):
        self.pair_copy().wait_recv()
        self.pacc[...] = self.mine[...] + self.ppair[...]
        for c in self.scatter1():
            c.start()

    def step2(self):
        r = self.r
        mine = self.pacc[pl.ds(r.me1 * r.n2, r.n2)]
        for d, c in enumerate(self.scatter1(), 1):
            c.wait_recv()
            mine = mine + self.pr1[d * r.n2 : (d + 1) * r.n2]
        self.p1[0 : r.n2] = mine
        for c in self.scatter2():
            c.start()

    def step3(self):
        r = self.r
        one = self.p1[pl.ds(r.me2, 1)]
        for d, c in enumerate(self.scatter2(), 1):
            c.wait_recv()
            one = one + self.pr2[d : d + 1]
        self.total[r.q, pl.ds(r.me1 * r.n2 + r.me2, 1)] = one
        for c in self.gather2(0):
            c.start()

    def step4(self):
        for c in self.gather2(1):
            c.wait_recv()
        for c in self.gather1(0):
            c.start()
        self.share_copy(0, True).start()

    def step5(self):
        for d, c in enumerate(self.gather1(1), 1):
            c.wait_recv()
            self.share_copy(d, True).start()

    def arrive(self):
        for d in range(self.r.n1):
            self.share_copy(d, False).wait_recv()

    def finish(self):
        self.pair_copy().wait_send()
        for c in self.scatter1() + self.scatter2() + self.gather2(0) + self.gather1(0):
            c.wait_send()
        for d in range(self.r.n1):
            self.share_copy(d, True).wait_send()


def line_greet(nx, ny, partner):
    mx, my = lax.axis_index("scanx"), lax.axis_index("scany")
    greet(
        [(True, partner)]
        + [(True, {"scanx": lax.rem(mx + d, nx)}) for d in range(1, nx)]
        + [(True, {"scany": lax.rem(my + d, ny)}) for d in range(1, ny)]
    )


def each(step):
    p = lax.axis_index("pos")
    for q in range(2):
        pl.when(p == q)(functools.partial(step, q))


def halo_kernel(nx, ny, spec, *refs):
    loaded, pad, kept = refs[:5], refs[5], refs[6:11]
    send, recv, local = refs[11:]
    tile = spec.shape[1]
    half = (pad.shape[1] - tile) // 2
    own = pl.ds(half, tile)
    partner = {"pos": 1 - lax.axis_index("pos")}
    loads = [pltpu.make_async_copy(spec, pad.at[:, own, own], local.at[0])]
    for i, (src, dst) in enumerate(zip(loaded, kept), 1):
        loads.append(pltpu.make_async_copy(src, dst, local.at[i]))
    for c in loads:
        c.start()
    roles = [Role(q, nx, ny) for q in range(2)]
    sides = roles[1].sides1 + roles[0].sides1
    greet([(True, partner)] + [(side.has, side.where) for side in sides])
    halos = [Halo(r, spec, pad, send, recv, partner) for r in roles]
    each(lambda q: halos[q].begin())
    for i, at in enumerate(
        (
            (slice(None), pl.ds(0, half)),
            (slice(None), pl.ds(half + tile, half)),
            (slice(None), slice(None), pl.ds(0, half)),
            (slice(None), slice(None), pl.ds(half + tile, half)),
        )
    ):

        @pl.when(jnp.logical_not(sides[i].has))
        def _(at=at):
            pad[at] = jnp.zeros(pad.at[at].shape, pad.dtype)

    def rest(q):
        halos[q].relay()
        halos[1 - q].arrive()
        halos[q].finish()

    each(rest)
    for c in loads:
        c.wait()


def step_kernel(offsets, pad, probe, amplitudes, table_a, table_b, grad, prob):
    m = probe.shape[1]
    tall, span = m + 8, m + 128
    pr, pi = probe[0], probe[1]
    grad[...] = jnp.zeros(grad.shape, grad.dtype)
    blank_rows = jnp.zeros((tall - m, m), jnp.float32)
    blank_cols = jnp.zeros((tall, span - m), jnp.float32)
    bf = jnp.bfloat16
    positions = amplitudes.shape[0]

    def place_at(j):
        row, col = offsets[j, 0], offsets[j, 1]
        row_in, col_in = lax.rem(row, 8), lax.rem(col, 128)
        rows = pl.ds(pl.multiple_of(row - row_in, 8), tall)
        cols = pl.ds(pl.multiple_of(col - col_in, 128), span)
        return row_in, col_in, rows, cols

    def place(j, k, term):
        row_in, col_in, rows, cols = place_at(j)
        moved = pltpu.roll(jnp.concatenate([term, blank_rows], 0), row_in, 0)
        moved = pltpu.roll(jnp.concatenate([moved, blank_cols], 1), col_in, 1)
        grad[k, rows, cols] = grad[k, rows, cols] + moved

    power = pr * pr + pi * pi
    for j in range(positions):
        place(j, 2, power)
    sum_r = sum_i = None
    for j in range(positions):
        row_in, col_in, rows, cols = place_at(j)

        def window(k):
            block = pad[k, rows, cols]
            block = pltpu.roll(block, lax.rem(span - col_in, span), 1)[:, :m]
            return pltpu.roll(block, lax.rem(tall - row_in, tall), 0)[:m]

        ar, ai = window(0), window(1)
        er = pr * ar - pi * ai
        ei = pr * ai + pi * ar
        left = dot(table_a[...], jnp.concatenate([er.astype(bf), ei.astype(bf)], 0)).astype(bf)
        far = dot(jnp.concatenate([left[:m], left[m:]], 1), table_b[...])
        fr, fi = far[:, :m], far[:, m:]
        ratio = amplitudes[j].astype(jnp.float32) / jnp.maximum(jnp.sqrt(fr * fr + fi * fi), 0.2)
        projected = jnp.concatenate([(fr * ratio).astype(bf), (fi * ratio).astype(bf)], 0)
        back_half = dot(table_b[...], projected).astype(bf)
        back = dot(jnp.concatenate([back_half[:m], back_half[m:]], 1), table_a[...])
        dr = back[:, :m] - er
        di = back[:, m:] - ei
        tr = ar * dr + ai * di
        ti = ar * di - ai * dr
        sum_r = tr if sum_r is None else sum_r + tr
        sum_i = ti if sum_i is None else sum_i + ti
        place(j, 0, pr * dr + pi * di)
        place(j, 1, pr * di - pi * dr)
    n, s, lanes = prob.shape[1:]
    for k, value in enumerate((sum_r, sum_i)):
        for c in range(n):
            r0, l0 = c * s % m, c * s // m * lanes
            prob[k, c] = value[r0 : r0 + s, l0 : l0 + lanes]


def reduce_kernel(nx, ny, *refs):
    grad, prob, core, icore, total = refs[:5]
    (pair, acc, xr1, xr2, zr1, zr2, ipair, iacc, ixr1, ixr2, izr1, izr2) = refs[5:17]
    (ppair, pacc, p1, pr1, pr2) = refs[17:22]
    (gsend, grecv, isend, irecv, psend, precv) = refs[22:]
    p = lax.axis_index("pos")
    partner = {"pos": 1 - p}
    line_greet(nx, ny, partner)
    roles = [Role(q, nx, ny) for q in range(2)]
    folds = [
        Fold(r, grad.at[r.q], grad.at[r.o], pair, acc, (xr1, xr2, zr1, zr2), core, gsend, grecv, partner)
        for r in roles
    ]
    lights = [
        Fold(
            r,
            grad.at[2, :, pl.ds(r.q, 1)],
            grad.at[2, :, pl.ds(r.o, 1)],
            ipair,
            iacc,
            (ixr1, ixr2, izr1, izr2),
            icore,
            isend,
            irecv,
            partner,
        )
        for r in roles
    ]
    probes = [
        ProbeSum(r, prob.at[r.q], prob.at[r.o], ppair, pacc, p1, pr1, pr2, total, psend, precv, partner)
        for r in roles
    ]

    def objects(q):
        probe_sum, fold, light = probes[q], folds[q], lights[q]
        probe_sum.begin()
        fold.begin()
        light.begin()
        probe_sum.step1()
        fold.add(0)
        fold.add(1)
        fold.send_rims(0)
        light.add(0)
        light.add(1)
        light.send_rims(0)
        fold.add(2)
        light.add(2)
        probe_sum.step2()
        fold.fold(0)
        fold.send_rims(1)
        light.fold(0)
        light.send_rims(1)
        probe_sum.step3()
        fold.fold(1)
        fold.share()
        light.fold(1)
        light.share()
        probe_sum.step4()
        light.arrive()
        fold.arrive()

    each(objects)
    def closing(q):
        probes[q].step5()
        probes[1 - q].arrive()
        lights[q].finish()
        folds[q].finish()
        probes[q].finish()

    each(closing)

def apply_kernel(step_size, core, light, total, pad, probe, new_spec, new_probe):
    tile = new_spec.shape[1]
    half = (pad.shape[1] - tile) // 2
    m = probe.shape[1]
    h = core.shape[3]
    for k in range(2):
        for g in range(2):
            for b in range(2):
                r0 = (2 * g + b) * h
                old = pad[k, half + r0 : half + r0 + h, half : half + tile]
                new_spec[k, r0 : r0 + h] = old + core[k, g, b] / (light[b, g, 0] + 1.0)
    n, s, lanes = total.shape[1:]
    for k in range(2):
        for c in range(n):
            rows = slice(c * s % m, c * s % m + s)
            cols = slice(c * s // m * lanes, c * s // m * lanes + lanes)
            new_probe[k, rows, cols] = probe[k, rows, cols] + total[k, c] * step_size


def tables(length):
    index = np.arange(length)
    angle = ((index[:, None] * index[None, :]) % length).astype(np.float32) * np.float32(2.0 * math.pi / length)
    scale = np.float32(1.0 / math.sqrt(length))
    c = np.cos(angle) * scale
    s = np.sin(angle) * scale
    a = np.block([[c, s], [-s, c]]).astype(jnp.bfloat16)
    b = np.block([[c, -s], [s, c]]).astype(jnp.bfloat16)
    return a, b


def shards(nx, ny, consts, specimen, probe_wave, amplitudes, offsets):
    m = probe_wave.shape[1]
    tile = specimen.shape[1]
    wide = tile + m
    f32 = jnp.float32
    vm = pl.BlockSpec(memory_space=VMEM)
    sm = pl.BlockSpec(memory_space=pltpu.SMEM)
    anywhere = pl.BlockSpec(memory_space=pl.ANY)
    dma = pltpu.SemaphoreType.DMA
    lanes = 128
    n = nx * ny
    s = m * m // lanes // n
    h = wide // 8
    most = max(nx, ny)
    positions = offsets.shape[0]
    shaped = VMEM
    held = (offsets, probe_wave, amplitudes, consts[0], consts[1])
    hbm = pl.BlockSpec(memory_space=pltpu.HBM)
    pad, *held = pl.pallas_call(
        functools.partial(halo_kernel, nx, ny),
        out_shape=[shaped((2, wide, wide), f32)] + [shaped(x.shape, x.dtype) for x in held],
        in_specs=[hbm] * 6,
        out_specs=[vm] * 6,
        scratch_shapes=[dma((16,)), dma((16,)), dma((6,))],
        compiler_params=pltpu.CompilerParams(vmem_limit_bytes=16 * 2**20, collective_id=0, has_side_effects=True),
        name="halo",
    )(*[pltpu.with_memory_space_constraint(x, pltpu.HBM) for x in (specimen, *held)])
    grad, prob = pl.pallas_call(
        step_kernel,
        out_shape=[
            jax.ShapeDtypeStruct((3, wide, wide), f32),
            jax.ShapeDtypeStruct((2, n, s, lanes), f32),
        ],
        in_specs=[sm] + [vm] * 5,
        out_specs=[vm, vm],
        compiler_params=pltpu.CompilerParams(vmem_limit_bytes=32 * 2**20),
        name="step",
    )(held[0], pad, *held[1:])

    def field(size):
        return [
            VMEM((4, size, h, wide), f32),
            VMEM((4, size, h, wide), f32),
            VMEM((2, 4, size, h, wide // 4), f32),
            VMEM((2, 2, size, h, wide // 4), f32),
            VMEM((2, size, h, wide), f32),
            VMEM((2, size, h, wide // 2), f32),
        ]

    step_size = 1.0 / math.sqrt(positions * n * 2)
    core, light, total = pl.pallas_call(
        functools.partial(reduce_kernel, nx, ny),
        out_shape=[
            shaped((2, 2, 2, h, wide // 2), f32),
            shaped((2, 2, 1, h, wide // 2), f32),
            shaped((2, n, s, lanes), f32),
        ],
        in_specs=[vm] * 2,
        out_specs=[vm, vm, vm],
        scratch_shapes=[
            *field(2),
            *field(1),
            VMEM((n, s, lanes), f32),
            VMEM((n, s, lanes), f32),
            VMEM((most, s, lanes), f32),
            VMEM((n, s, lanes), f32),
            VMEM((most, s, lanes), f32),
            dma((8,)),
            dma((8,)),
            dma((8,)),
            dma((8,)),
            dma((6, most)),
            dma((6, most)),
        ],
        compiler_params=pltpu.CompilerParams(vmem_limit_bytes=32 * 2**20, collective_id=1, has_side_effects=True),
        name="reduce",
    )(grad.reshape(3, 4, 2, h, wide), prob)
    return pl.pallas_call(
        functools.partial(apply_kernel, step_size),
        out_shape=[
            jax.ShapeDtypeStruct(specimen.shape, f32),
            jax.ShapeDtypeStruct(probe_wave.shape, f32),
        ],
        in_specs=[vm] * 5,
        out_specs=[vm, vm],
        compiler_params=pltpu.CompilerParams(vmem_limit_bytes=16 * 2**20),
        name="apply",
    )(core, light, total, pad, held[1])


def solution(mesh):
    nx, ny = mesh.shape["scanx"], mesh.shape["scany"]

    def run(specimen, probe_wave, amplitudes, offsets):
        consts = tables(probe_wave.shape[2])
        return jax.shard_map(
            lambda *args: shards(nx, ny, [jnp.asarray(t) for t in consts], *args),
            mesh=mesh,
            in_specs=(
                P(None, ("groups", "scanx"), "scany"),
                P(None, "groups", None),
                P(("groups", "scanx", "scany", "pos"), None, None),
                P(("groups", "scanx", "scany", "pos"), None),
            ),
            out_specs=(P(None, ("groups", "scanx"), "scany"), P(None, "groups", None)),
            check_vma=False,
        )(specimen, probe_wave, amplitudes, offsets)

    return run
```

```python
import functools
import math

import jax
import jax.numpy as jnp
import numpy as np
from jax import lax
from jax.experimental import pallas as pl
from jax.experimental.pallas import tpu as pltpu
from jax.sharding import PartitionSpec as P

MESH = pl.DeviceIdType.MESH
VMEM = pltpu.VMEM


def remote(src, dst, send, recv, where):
    return pltpu.make_async_remote_copy(
        src_ref=src, dst_ref=dst, send_sem=send, recv_sem=recv, device_id=where, device_id_type=MESH
    )


def greet(conditions_devices):
    barrier = pltpu.get_barrier_semaphore()
    for present, where in conditions_devices:
        if present is True:
            pl.semaphore_signal(barrier, inc=1, device_id=where, device_id_type=MESH)
        else:

            @pl.when(present)
            def _(where=where):
                pl.semaphore_signal(barrier, inc=1, device_id=where, device_id_type=MESH)

    fixed = sum(1 for present, _ in conditions_devices if present is True)
    peers = [present.astype(jnp.int32) for present, _ in conditions_devices if present is not True]
    pl.semaphore_wait(barrier, sum(peers, fixed))


class Side:
    def __init__(self, axis, count, step):
        me = lax.axis_index(axis)
        self.has = me > 0 if step < 0 else me < count - 1
        self.where = {axis: me + step}


class Role:
    def __init__(self, q, nx, ny):
        along_x = ("scanx", nx, Side("scanx", nx, -1), Side("scanx", nx, 1))
        along_y = ("scany", ny, Side("scany", ny, -1), Side("scany", ny, 1))
        one, two = (along_y, along_x) if q == 0 else (along_x, along_y)
        self.q, self.o, self.rows_first = q, 1 - q, q == 1
        self.axis1, self.n1, self.sides1 = one[0], one[1], one[2:]
        self.axis2, self.n2, self.sides2 = two[0], two[1], two[2:]
        self.me1, self.me2 = lax.axis_index(self.axis1), lax.axis_index(self.axis2)


def when(*conditions):
    return pl.when(functools.reduce(jnp.logical_and, conditions))


def dot(a, b):
    return jnp.dot(a, b, preferred_element_type=jnp.float32)


class Halo:
    def __init__(self, role, spec, pad, send, recv, partner):
        self.r, self.spec, self.pad, self.partner = role, spec, pad, partner
        self.send, self.recv = send, recv
        tile = spec.shape[1]
        half = (pad.shape[1] - tile) // 2
        self.own = pl.ds(half, tile)
        self.margins = (pl.ds(0, half), pl.ds(half + tile, half))
        self.edges = (pl.ds(0, half), pl.ds(tile - half, half))
        self.pad_edges = (pl.ds(half, half), pl.ds(tile, half))
        self.whole = pl.ds(0, tile)

    def at(self, one, two):
        return (self.r.q, one, two) if self.r.rows_first else (self.r.q, two, one)

    def copy(self, src, dst, i, where):
        return remote(src, dst, self.send.at[i], self.recv.at[i], where)

    def strip1(self, m):
        return self.copy(
            self.spec.at[self.at(self.edges[1 - m], self.whole)],
            self.pad.at[self.at(self.margins[m], self.own)],
            m,
            self.r.sides1[1 - m].where,
        )

    def strip2(self, m):
        return self.copy(
            self.spec.at[self.at(self.whole, self.edges[1 - m])],
            self.pad.at[self.at(self.own, self.margins[m])],
            2 + m,
            self.r.sides2[1 - m].where,
        )

    def corner(self, m1, m2):
        return self.copy(
            self.pad.at[self.at(self.margins[m1], self.pad_edges[1 - m2])],
            self.pad.at[self.at(self.margins[m1], self.margins[m2])],
            4 + 2 * m1 + m2,
            self.r.sides2[1 - m2].where,
        )

    def share(self, i, one, two):
        ref = self.pad.at[self.at(one, two)]
        return self.copy(ref, ref, 8 + i, self.partner)

    def share1(self, m):
        return self.share(m, self.margins[m], self.own)

    def share2(self, m):
        return self.share(2 + m, self.own, self.margins[m])

    def share_corner(self, m1, m2):
        return self.share(4 + 2 * m1 + m2, self.margins[m1], self.margins[m2])

    def begin(self):
        for m in range(2):
            when(self.r.sides1[1 - m].has)(self.strip1(m).start)
        for m in range(2):
            when(self.r.sides2[1 - m].has)(self.strip2(m).start)

    def relay(self):
        r = self.r
        for m1 in range(2):

            @when(r.sides1[m1].has)
            def _():
                self.strip1(m1).wait_recv()
                for m2 in range(2):
                    when(r.sides2[1 - m2].has)(self.corner(m1, m2).start)
                self.share1(m1).start()

        for m in range(2):

            @when(r.sides2[m].has)
            def _():
                self.strip2(m).wait_recv()
                self.share2(m).start()

        for m1 in range(2):
            for m2 in range(2):

                @when(r.sides1[m1].has, r.sides2[m2].has)
                def _():
                    self.corner(m1, m2).wait_recv()
                    self.share_corner(m1, m2).start()

    def arrive(self):
        r = self.r
        for m in range(2):
            when(r.sides1[m].has)(self.share1(m).wait_recv)
            when(r.sides2[m].has)(self.share2(m).wait_recv)
        for m1 in range(2):
            for m2 in range(2):
                when(r.sides1[m1].has, r.sides2[m2].has)(self.share_corner(m1, m2).wait_recv)

    def finish(self):
        r = self.r
        for m in range(2):
            when(r.sides1[1 - m].has)(self.strip1(m).wait_send)
            when(r.sides2[1 - m].has)(self.strip2(m).wait_send)
            when(r.sides1[m].has)(self.share1(m).wait_send)
            when(r.sides2[m].has)(self.share2(m).wait_send)
        for m1 in range(2):
            for m2 in range(2):
                when(r.sides1[m1].has, r.sides2[1 - m2].has)(self.corner(m1, m2).wait_send)
                when(r.sides1[m1].has, r.sides2[m2].has)(self.share_corner(m1, m2).wait_send)


class Fold:
    def __init__(self, role, mine, theirs, pair, acc, rims, core, send, recv, partner):
        self.r, self.mine, self.theirs, self.pair, self.acc = role, mine, theirs, pair, acc
        self.xr1, self.xr2, self.zr1, self.zr2 = rims
        self.core, self.send, self.recv, self.partner = core, send, recv, partner
        w = acc.shape[-1]
        self.w, self.q4 = w, w // 4

    def pieces(self, rows):
        q4, w = self.q4, self.w
        if rows:
            return [(pl.ds(0, 1),), (pl.ds(3, 1),), (pl.ds(1, 2),)]
        lead = (slice(None),) * 3
        return [lead + (pl.ds(0, q4),), lead + (pl.ds(3 * q4, q4),), lead + (pl.ds(q4, 2 * q4),)]

    def pair_copy(self, i, rows):
        at = self.pieces(rows)[i]
        return remote(self.theirs.at[at], self.pair.at[at], self.send.at[i], self.recv.at[i], self.partner)

    def begin(self):
        for i in range(3):
            self.pair_copy(i, not self.r.rows_first).start()

    def add(self, i):
        self.pair_copy(i, self.r.rows_first).wait_recv()
        at = self.pieces(self.r.rows_first)[i]
        self.acc[at] = self.mine[at] + self.pair[at]

    def rim_copy(self, stage, m):
        r, q4, w = self.r, self.q4, self.w
        rows = r.rows_first == (stage == 0)
        k = 1 - m
        if rows:
            cols = pl.ds(0, w) if stage == 0 else pl.ds(q4, 2 * q4)
            src = self.acc.at[3 * k, :, :, cols]
            rim = self.zr1 if stage == 0 else self.zr2
        else:
            groups = pl.ds(0, 4) if stage == 0 else pl.ds(1, 2)
            src = self.acc.at[groups, :, :, pl.ds(3 * k * q4, q4)]
            rim = self.xr1 if stage == 0 else self.xr2
        sides = r.sides1 if stage == 0 else r.sides2
        i = 3 + 2 * stage + m
        return remote(src, rim.at[m], self.send.at[i], self.recv.at[i], sides[k].where)

    def send_rims(self, stage):
        sides = self.r.sides1 if stage == 0 else self.r.sides2
        for m in range(2):
            when(sides[1 - m].has)(self.rim_copy(stage, m).start)

    def fold(self, stage):
        r, q4, w, acc = self.r, self.q4, self.w, self.acc
        rows = r.rows_first == (stage == 0)
        sides = r.sides1 if stage == 0 else r.sides2
        for m in range(2):

            @when(sides[m].has)
            def _():
                self.rim_copy(stage, m).wait_recv()
                if rows:
                    cols = pl.ds(0, w) if stage == 0 else pl.ds(q4, 2 * q4)
                    rim = self.zr1 if stage == 0 else self.zr2
                    acc[1 + m, :, :, cols] = acc[1 + m, :, :, cols] + rim[m]
                else:
                    groups = pl.ds(0, 4) if stage == 0 else pl.ds(1, 2)
                    cols = pl.ds((1 + m) * q4, q4)
                    rim = self.xr1 if stage == 0 else self.xr2
                    acc[groups, :, :, cols] = acc[groups, :, :, cols] + rim[m]

    def share_copy(self, q):
        return remote(self.core.at[q], self.core.at[q], self.send.at[7], self.recv.at[7], self.partner)

    def share(self):
        q4 = self.q4
        self.core[self.r.q] = self.acc[1:3, :, :, q4 : 3 * q4]
        self.share_copy(self.r.q).start()

    def arrive(self):
        self.share_copy(self.r.o).wait_recv()

    def finish(self):
        r = self.r
        for i in range(3):
            self.pair_copy(i, not r.rows_first).wait_send()
        for m in range(2):
            when(r.sides1[1 - m].has)(self.rim_copy(0, m).wait_send)
            when(r.sides2[1 - m].has)(self.rim_copy(1, m).wait_send)
        self.share_copy(r.q).wait_send()


class ProbeSum:
    def __init__(self, role, mine, theirs, ppair, pacc, p1, pr1, pr2, total, send, recv, partner):
        self.r, self.mine, self.theirs = role, mine, theirs
        self.ppair, self.pacc, self.p1 = ppair, pacc, p1
        self.pr1, self.pr2, self.total = pr1, pr2, total
        self.send, self.recv, self.partner = send, recv, partner

    def copy(self, src, dst, stage, d, where):
        return remote(src, dst, self.send.at[stage, d], self.recv.at[stage, d], where)

    def pair_copy(self):
        return self.copy(self.theirs, self.ppair, 0, 0, self.partner)

    def begin(self):
        self.pair_copy().start()

    def scatter1(self):
        r = self.r
        out = []
        for d in range(1, r.n1):
            j = lax.rem(r.me1 + d, r.n1)
            src = self.pacc.at[pl.ds(j * r.n2, r.n2)]
            out.append(self.copy(src, self.pr1.at[pl.ds(d * r.n2, r.n2)], 1, d, {r.axis1: j}))
        return out

    def scatter2(self):
        r = self.r
        out = []
        for d in range(1, r.n2):
            j = lax.rem(r.me2 + d, r.n2)
            out.append(self.copy(self.p1.at[pl.ds(j, 1)], self.pr2.at[pl.ds(d, 1)], 2, d, {r.axis2: j}))
        return out

    def gather2(self, back):
        r = self.r
        out = []
        for d in range(1, r.n2):
            j = lax.rem(r.me2 + d, r.n2)
            origin = lax.rem(r.me2 - d + r.n2, r.n2) if back else r.me2
            ref = self.total.at[r.q, pl.ds(r.me1 * r.n2 + origin, 1)]
            out.append(self.copy(ref, ref, 3, d, {r.axis2: j}))
        return out

    def gather1(self, back):
        r = self.r
        out = []
        for d in range(1, r.n1):
            j = lax.rem(r.me1 + d, r.n1)
            origin = lax.rem(r.me1 - d + r.n1, r.n1) if back else r.me1
            ref = self.total.at[r.q, pl.ds(origin * r.n2, r.n2)]
            out.append(self.copy(ref, ref, 4, d, {r.axis1: j}))
        return out

    def share_copy(self, d, sender):
        r = self.r
        origin = lax.rem(r.me1 - d + r.n1, r.n1)
        ref = self.total.at[r.q, pl.ds(origin * r.n2, r.n2)]
        return self.copy(ref, ref, 5, d, self.partner)

    def step1(self):
        self.pair_copy().wait_recv()
        self.pacc[...] = self.mine[...] + self.ppair[...]
        for c in self.scatter1():
            c.start()

    def step2(self):
        r = self.r
        mine = self.pacc[pl.ds(r.me1 * r.n2, r.n2)]
        for d, c in enumerate(self.scatter1(), 1):
            c.wait_recv()
            mine = mine + self.pr1[d * r.n2 : (d + 1) * r.n2]
        self.p1[0 : r.n2] = mine
        for c in self.scatter2():
            c.start()

    def step3(self):
        r = self.r
        one = self.p1[pl.ds(r.me2, 1)]
        for d, c in enumerate(self.scatter2(), 1):
            c.wait_recv()
            one = one + self.pr2[d : d + 1]
        self.total[r.q, pl.ds(r.me1 * r.n2 + r.me2, 1)] = one
        for c in self.gather2(0):
            c.start()

    def step4(self):
        for c in self.gather2(1):
            c.wait_recv()
        for c in self.gather1(0):
            c.start()
        self.share_copy(0, True).start()

    def step5(self):
        for d, c in enumerate(self.gather1(1), 1):
            c.wait_recv()
            self.share_copy(d, True).start()

    def arrive(self):
        for d in range(self.r.n1):
            self.share_copy(d, False).wait_recv()

    def finish(self):
        self.pair_copy().wait_send()
        for c in self.scatter1() + self.scatter2() + self.gather2(0) + self.gather1(0):
            c.wait_send()
        for d in range(self.r.n1):
            self.share_copy(d, True).wait_send()


def line_greet(nx, ny, partner):
    mx, my = lax.axis_index("scanx"), lax.axis_index("scany")
    greet(
        [(True, partner)]
        + [(True, {"scanx": lax.rem(mx + d, nx)}) for d in range(1, nx)]
        + [(True, {"scany": lax.rem(my + d, ny)}) for d in range(1, ny)]
    )


def each(step):
    p = lax.axis_index("pos")
    for q in range(2):
        pl.when(p == q)(functools.partial(step, q))


def halo_kernel(nx, ny, spec, *refs):
    loaded, pad, kept = refs[:5], refs[5], refs[6:11]
    send, recv, local = refs[11:]
    tile = spec.shape[1]
    half = (pad.shape[1] - tile) // 2
    own = pl.ds(half, tile)
    partner = {"pos": 1 - lax.axis_index("pos")}
    loads = [pltpu.make_async_copy(spec, pad.at[:, own, own], local.at[0])]
    for i, (src, dst) in enumerate(zip(loaded, kept), 1):
        loads.append(pltpu.make_async_copy(src, dst, local.at[i]))
    for c in loads:
        c.start()
    roles = [Role(q, nx, ny) for q in range(2)]
    sides = roles[1].sides1 + roles[0].sides1
    greet([(True, partner)] + [(side.has, side.where) for side in sides])
    halos = [Halo(r, spec, pad, send, recv, partner) for r in roles]
    each(lambda q: halos[q].begin())
    for i, at in enumerate(
        (
            (slice(None), pl.ds(0, half)),
            (slice(None), pl.ds(half + tile, half)),
            (slice(None), slice(None), pl.ds(0, half)),
            (slice(None), slice(None), pl.ds(half + tile, half)),
        )
    ):

        @pl.when(jnp.logical_not(sides[i].has))
        def _(at=at):
            pad[at] = jnp.zeros(pad.at[at].shape, pad.dtype)

    def rest(q):
        halos[q].relay()
        halos[1 - q].arrive()
        halos[q].finish()

    each(rest)
    for c in loads:
        c.wait()


def step_kernel(offsets, pad, probe, amplitudes, table_a, table_b, grad, prob):
    m = probe.shape[1]
    tall, span = m + 8, m + 128
    pr, pi = probe[0], probe[1]
    grad[...] = jnp.zeros(grad.shape, grad.dtype)
    blank_rows = jnp.zeros((tall - m, m), jnp.float32)
    blank_cols = jnp.zeros((tall, span - m), jnp.float32)
    bf = jnp.bfloat16
    positions = amplitudes.shape[0]

    def place_at(j):
        row, col = offsets[j, 0], offsets[j, 1]
        row_in, col_in = lax.rem(row, 8), lax.rem(col, 128)
        rows = pl.ds(pl.multiple_of(row - row_in, 8), tall)
        cols = pl.ds(pl.multiple_of(col - col_in, 128), span)
        return row_in, col_in, rows, cols

    def place(j, k, term):
        row_in, col_in, rows, cols = place_at(j)
        moved = pltpu.roll(jnp.concatenate([term, blank_rows], 0), row_in, 0)
        moved = pltpu.roll(jnp.concatenate([moved, blank_cols], 1), col_in, 1)
        grad[k, rows, cols] = grad[k, rows, cols] + moved

    power = pr * pr + pi * pi
    for j in range(positions):
        place(j, 2, power)
    sum_r = sum_i = None
    for j in range(positions):
        row_in, col_in, rows, cols = place_at(j)

        def window(k):
            block = pad[k, rows, cols]
            block = pltpu.roll(block, lax.rem(span - col_in, span), 1)[:, :m]
            return pltpu.roll(block, lax.rem(tall - row_in, tall), 0)[:m]

        ar, ai = window(0), window(1)
        er = pr * ar - pi * ai
        ei = pr * ai + pi * ar
        left = dot(table_a[...], jnp.concatenate([er.astype(bf), ei.astype(bf)], 0)).astype(bf)
        far = dot(jnp.concatenate([left[:m], left[m:]], 1), table_b[...])
        fr, fi = far[:, :m], far[:, m:]
        ratio = amplitudes[j].astype(jnp.float32) / jnp.maximum(jnp.sqrt(fr * fr + fi * fi), 0.2)
        projected = jnp.concatenate([(fr * ratio).astype(bf), (fi * ratio).astype(bf)], 0)
        back_half = dot(table_b[...], projected).astype(bf)
        back = dot(jnp.concatenate([back_half[:m], back_half[m:]], 1), table_a[...])
        dr = back[:, :m] - er
        di = back[:, m:] - ei
        tr = ar * dr + ai * di
        ti = ar * di - ai * dr
        sum_r = tr if sum_r is None else sum_r + tr
        sum_i = ti if sum_i is None else sum_i + ti
        place(j, 0, pr * dr + pi * di)
        place(j, 1, pr * di - pi * dr)
    n, s, lanes = prob.shape[1:]
    for k, value in enumerate((sum_r, sum_i)):
        for c in range(n):
            r0, l0 = c * s % m, c * s // m * lanes
            prob[k, c] = value[r0 : r0 + s, l0 : l0 + lanes]


def reduce_kernel(nx, ny, *refs):
    grad, prob, core, icore, total = refs[:5]
    (pair, acc, xr1, xr2, zr1, zr2, ipair, iacc, ixr1, ixr2, izr1, izr2) = refs[5:17]
    (ppair, pacc, p1, pr1, pr2) = refs[17:22]
    (gsend, grecv, isend, irecv, psend, precv) = refs[22:]
    p = lax.axis_index("pos")
    partner = {"pos": 1 - p}
    line_greet(nx, ny, partner)
    roles = [Role(q, nx, ny) for q in range(2)]
    folds = [
        Fold(r, grad.at[r.q], grad.at[r.o], pair, acc, (xr1, xr2, zr1, zr2), core, gsend, grecv, partner)
        for r in roles
    ]
    lights = [
        Fold(
            r,
            grad.at[2, :, pl.ds(r.q, 1)],
            grad.at[2, :, pl.ds(r.o, 1)],
            ipair,
            iacc,
            (ixr1, ixr2, izr1, izr2),
            icore,
            isend,
            irecv,
            partner,
        )
        for r in roles
    ]
    probes = [
        ProbeSum(r, prob.at[r.q], prob.at[r.o], ppair, pacc, p1, pr1, pr2, total, psend, precv, partner)
        for r in roles
    ]

    def objects(q):
        probe_sum, fold, light = probes[q], folds[q], lights[q]
        probe_sum.begin()
        fold.begin()
        light.begin()
        probe_sum.step1()
        fold.add(0)
        fold.add(1)
        fold.send_rims(0)
        fold.add(2)
        for i in range(3):
            light.add(i)
        probe_sum.step2()
        light.send_rims(0)
        fold.fold(0)
        fold.send_rims(1)
        probe_sum.step3()
        light.fold(0)
        light.send_rims(1)
        probe_sum.step4()
        fold.fold(1)
        fold.share()
        light.fold(1)
        light.share()
        probe_sum.step5()
        light.arrive()
        fold.arrive()

    each(objects)
    def closing(q):
        probes[1 - q].arrive()
        lights[q].finish()
        folds[q].finish()
        probes[q].finish()

    each(closing)

def apply_kernel(step_size, core, light, total, pad, probe, new_spec, new_probe):
    tile = new_spec.shape[1]
    half = (pad.shape[1] - tile) // 2
    m = probe.shape[1]
    h = core.shape[3]
    for k in range(2):
        for g in range(2):
            for b in range(2):
                r0 = (2 * g + b) * h
                old = pad[k, half + r0 : half + r0 + h, half : half + tile]
                new_spec[k, r0 : r0 + h] = old + core[k, g, b] / (light[b, g, 0] + 1.0)
    n, s, lanes = total.shape[1:]
    for k in range(2):
        for c in range(n):
            rows = slice(c * s % m, c * s % m + s)
            cols = slice(c * s // m * lanes, c * s // m * lanes + lanes)
            new_probe[k, rows, cols] = probe[k, rows, cols] + total[k, c] * step_size


def tables(length):
    index = np.arange(length)
    angle = ((index[:, None] * index[None, :]) % length).astype(np.float32) * np.float32(2.0 * math.pi / length)
    scale = np.float32(1.0 / math.sqrt(length))
    c = np.cos(angle) * scale
    s = np.sin(angle) * scale
    a = np.block([[c, s], [-s, c]]).astype(jnp.bfloat16)
    b = np.block([[c, -s], [s, c]]).astype(jnp.bfloat16)
    return a, b


def shards(nx, ny, consts, specimen, probe_wave, amplitudes, offsets):
    m = probe_wave.shape[1]
    tile = specimen.shape[1]
    wide = tile + m
    f32 = jnp.float32
    vm = pl.BlockSpec(memory_space=VMEM)
    sm = pl.BlockSpec(memory_space=pltpu.SMEM)
    anywhere = pl.BlockSpec(memory_space=pl.ANY)
    dma = pltpu.SemaphoreType.DMA
    lanes = 128
    n = nx * ny
    s = m * m // lanes // n
    h = wide // 8
    most = max(nx, ny)
    positions = offsets.shape[0]
    shaped = VMEM
    held = (offsets, probe_wave, amplitudes, consts[0], consts[1])
    hbm = pl.BlockSpec(memory_space=pltpu.HBM)
    pad, *held = pl.pallas_call(
        functools.partial(halo_kernel, nx, ny),
        out_shape=[shaped((2, wide, wide), f32)] + [shaped(x.shape, x.dtype) for x in held],
        in_specs=[hbm] * 6,
        out_specs=[vm] * 6,
        scratch_shapes=[dma((16,)), dma((16,)), dma((6,))],
        compiler_params=pltpu.CompilerParams(vmem_limit_bytes=16 * 2**20, collective_id=0, has_side_effects=True),
        name="halo",
    )(*[pltpu.with_memory_space_constraint(x, pltpu.HBM) for x in (specimen, *held)])
    grad, prob = pl.pallas_call(
        step_kernel,
        out_shape=[
            jax.ShapeDtypeStruct((3, wide, wide), f32),
            jax.ShapeDtypeStruct((2, n, s, lanes), f32),
        ],
        in_specs=[sm] + [vm] * 5,
        out_specs=[vm, vm],
        compiler_params=pltpu.CompilerParams(vmem_limit_bytes=32 * 2**20),
        name="step",
    )(held[0], pad, *held[1:])

    def field(size):
        return [
            VMEM((4, size, h, wide), f32),
            VMEM((4, size, h, wide), f32),
            VMEM((2, 4, size, h, wide // 4), f32),
            VMEM((2, 2, size, h, wide // 4), f32),
            VMEM((2, size, h, wide), f32),
            VMEM((2, size, h, wide // 2), f32),
        ]

    step_size = 1.0 / math.sqrt(positions * n * 2)
    core, light, total = pl.pallas_call(
        functools.partial(reduce_kernel, nx, ny),
        out_shape=[
            shaped((2, 2, 2, h, wide // 2), f32),
            shaped((2, 2, 1, h, wide // 2), f32),
            shaped((2, n, s, lanes), f32),
        ],
        in_specs=[vm] * 2,
        out_specs=[vm, vm, vm],
        scratch_shapes=[
            *field(2),
            *field(1),
            VMEM((n, s, lanes), f32),
            VMEM((n, s, lanes), f32),
            VMEM((most, s, lanes), f32),
            VMEM((n, s, lanes), f32),
            VMEM((most, s, lanes), f32),
            dma((8,)),
            dma((8,)),
            dma((8,)),
            dma((8,)),
            dma((6, most)),
            dma((6, most)),
        ],
        compiler_params=pltpu.CompilerParams(vmem_limit_bytes=32 * 2**20, collective_id=1, has_side_effects=True),
        name="reduce",
    )(grad.reshape(3, 4, 2, h, wide), prob)
    return pl.pallas_call(
        functools.partial(apply_kernel, step_size),
        out_shape=[
            jax.ShapeDtypeStruct(specimen.shape, f32),
            jax.ShapeDtypeStruct(probe_wave.shape, f32),
        ],
        in_specs=[vm] * 5,
        out_specs=[vm, vm],
        compiler_params=pltpu.CompilerParams(vmem_limit_bytes=16 * 2**20),
        name="apply",
    )(core, light, total, pad, held[1])


def solution(mesh):
    nx, ny = mesh.shape["scanx"], mesh.shape["scany"]

    def run(specimen, probe_wave, amplitudes, offsets):
        consts = tables(probe_wave.shape[2])
        return jax.shard_map(
            lambda *args: shards(nx, ny, [jnp.asarray(t) for t in consts], *args),
            mesh=mesh,
            in_specs=(
                P(None, ("groups", "scanx"), "scany"),
                P(None, "groups", None),
                P(("groups", "scanx", "scany", "pos"), None, None),
                P(("groups", "scanx", "scany", "pos"), None),
            ),
            out_specs=(P(None, ("groups", "scanx"), "scany"), P(None, "groups", None)),
            check_vma=False,
        )(specimen, probe_wave, amplitudes, offsets)

    return run
```

```python
import functools
import math

import jax
import jax.numpy as jnp
import numpy as np
from jax import lax
from jax.experimental import pallas as pl
from jax.experimental.pallas import tpu as pltpu
from jax.sharding import PartitionSpec as P

MESH = pl.DeviceIdType.MESH
VMEM = pltpu.VMEM


def remote(src, dst, send, recv, where):
    return pltpu.make_async_remote_copy(
        src_ref=src, dst_ref=dst, send_sem=send, recv_sem=recv, device_id=where, device_id_type=MESH
    )


def greet(conditions_devices):
    barrier = pltpu.get_barrier_semaphore()
    for present, where in conditions_devices:
        if present is True:
            pl.semaphore_signal(barrier, inc=1, device_id=where, device_id_type=MESH)
        else:

            @pl.when(present)
            def _(where=where):
                pl.semaphore_signal(barrier, inc=1, device_id=where, device_id_type=MESH)

    fixed = sum(1 for present, _ in conditions_devices if present is True)
    peers = [present.astype(jnp.int32) for present, _ in conditions_devices if present is not True]
    pl.semaphore_wait(barrier, sum(peers, fixed))


class Side:
    def __init__(self, axis, count, step):
        me = lax.axis_index(axis)
        self.has = me > 0 if step < 0 else me < count - 1
        self.where = {axis: me + step}


class Role:
    def __init__(self, q, nx, ny):
        along_x = ("scanx", nx, Side("scanx", nx, -1), Side("scanx", nx, 1))
        along_y = ("scany", ny, Side("scany", ny, -1), Side("scany", ny, 1))
        one, two = (along_y, along_x) if q == 0 else (along_x, along_y)
        self.q, self.o, self.rows_first = q, 1 - q, q == 1
        self.axis1, self.n1, self.sides1 = one[0], one[1], one[2:]
        self.axis2, self.n2, self.sides2 = two[0], two[1], two[2:]
        self.me1, self.me2 = lax.axis_index(self.axis1), lax.axis_index(self.axis2)


def when(*conditions):
    return pl.when(functools.reduce(jnp.logical_and, conditions))


def dot(a, b):
    return jnp.dot(a, b, preferred_element_type=jnp.float32)


class Halo:
    def __init__(self, role, spec, pad, send, recv, partner):
        self.r, self.spec, self.pad, self.partner = role, spec, pad, partner
        self.send, self.recv = send, recv
        tile = spec.shape[1]
        half = (pad.shape[1] - tile) // 2
        self.own = pl.ds(half, tile)
        self.margins = (pl.ds(0, half), pl.ds(half + tile, half))
        self.edges = (pl.ds(0, half), pl.ds(tile - half, half))
        self.pad_edges = (pl.ds(half, half), pl.ds(tile, half))
        self.whole = pl.ds(0, tile)

    def at(self, one, two):
        return (self.r.q, one, two) if self.r.rows_first else (self.r.q, two, one)

    def copy(self, src, dst, i, where):
        return remote(src, dst, self.send.at[i], self.recv.at[i], where)

    def strip1(self, m):
        return self.copy(
            self.spec.at[self.at(self.edges[1 - m], self.whole)],
            self.pad.at[self.at(self.margins[m], self.own)],
            m,
            self.r.sides1[1 - m].where,
        )

    def strip2(self, m):
        return self.copy(
            self.spec.at[self.at(self.whole, self.edges[1 - m])],
            self.pad.at[self.at(self.own, self.margins[m])],
            2 + m,
            self.r.sides2[1 - m].where,
        )

    def corner(self, m1, m2):
        return self.copy(
            self.pad.at[self.at(self.margins[m1], self.pad_edges[1 - m2])],
            self.pad.at[self.at(self.margins[m1], self.margins[m2])],
            4 + 2 * m1 + m2,
            self.r.sides2[1 - m2].where,
        )

    def share(self, i, one, two):
        ref = self.pad.at[self.at(one, two)]
        return self.copy(ref, ref, 8 + i, self.partner)

    def share1(self, m):
        return self.share(m, self.margins[m], self.own)

    def share2(self, m):
        return self.share(2 + m, self.own, self.margins[m])

    def share_corner(self, m1, m2):
        return self.share(4 + 2 * m1 + m2, self.margins[m1], self.margins[m2])

    def begin(self):
        for m in range(2):
            when(self.r.sides1[1 - m].has)(self.strip1(m).start)
        for m in range(2):
            when(self.r.sides2[1 - m].has)(self.strip2(m).start)

    def relay(self):
        r = self.r
        for m1 in range(2):

            @when(r.sides1[m1].has)
            def _():
                self.strip1(m1).wait_recv()
                for m2 in range(2):
                    when(r.sides2[1 - m2].has)(self.corner(m1, m2).start)
                self.share1(m1).start()

        for m in range(2):

            @when(r.sides2[m].has)
            def _():
                self.strip2(m).wait_recv()
                self.share2(m).start()

        for m1 in range(2):
            for m2 in range(2):

                @when(r.sides1[m1].has, r.sides2[m2].has)
                def _():
                    self.corner(m1, m2).wait_recv()
                    self.share_corner(m1, m2).start()

    def arrive(self):
        r = self.r
        for m in range(2):
            when(r.sides1[m].has)(self.share1(m).wait_recv)
            when(r.sides2[m].has)(self.share2(m).wait_recv)
        for m1 in range(2):
            for m2 in range(2):
                when(r.sides1[m1].has, r.sides2[m2].has)(self.share_corner(m1, m2).wait_recv)

    def finish(self):
        r = self.r
        for m in range(2):
            when(r.sides1[1 - m].has)(self.strip1(m).wait_send)
            when(r.sides2[1 - m].has)(self.strip2(m).wait_send)
            when(r.sides1[m].has)(self.share1(m).wait_send)
            when(r.sides2[m].has)(self.share2(m).wait_send)
        for m1 in range(2):
            for m2 in range(2):
                when(r.sides1[m1].has, r.sides2[1 - m2].has)(self.corner(m1, m2).wait_send)
                when(r.sides1[m1].has, r.sides2[m2].has)(self.share_corner(m1, m2).wait_send)


class Fold:
    def __init__(self, role, mine, theirs, pair, acc, rims, core, send, recv, partner):
        self.r, self.mine, self.theirs, self.pair, self.acc = role, mine, theirs, pair, acc
        self.xr1, self.xr2, self.zr1, self.zr2 = rims
        self.core, self.send, self.recv, self.partner = core, send, recv, partner
        w = acc.shape[-1]
        self.w, self.q4 = w, w // 4

    def pieces(self, rows):
        q4, w = self.q4, self.w
        if rows:
            return [(pl.ds(0, 1),), (pl.ds(3, 1),), (pl.ds(1, 2),)]
        lead = (slice(None),) * 3
        return [lead + (pl.ds(0, q4),), lead + (pl.ds(3 * q4, q4),), lead + (pl.ds(q4, 2 * q4),)]

    def pair_copy(self, i, rows):
        at = self.pieces(rows)[i]
        return remote(self.theirs.at[at], self.pair.at[at], self.send.at[i], self.recv.at[i], self.partner)

    def begin(self):
        for i in range(3):
            self.pair_copy(i, not self.r.rows_first).start()

    def add(self, i):
        self.pair_copy(i, self.r.rows_first).wait_recv()
        at = self.pieces(self.r.rows_first)[i]
        self.acc[at] = self.mine[at] + self.pair[at]

    def rim_copy(self, stage, m):
        r, q4, w = self.r, self.q4, self.w
        rows = r.rows_first == (stage == 0)
        k = 1 - m
        if rows:
            cols = pl.ds(0, w) if stage == 0 else pl.ds(q4, 2 * q4)
            src = self.acc.at[3 * k, :, :, cols]
            rim = self.zr1 if stage == 0 else self.zr2
        else:
            groups = pl.ds(0, 4) if stage == 0 else pl.ds(1, 2)
            src = self.acc.at[groups, :, :, pl.ds(3 * k * q4, q4)]
            rim = self.xr1 if stage == 0 else self.xr2
        sides = r.sides1 if stage == 0 else r.sides2
        i = 3 + 2 * stage + m
        return remote(src, rim.at[m], self.send.at[i], self.recv.at[i], sides[k].where)

    def send_rims(self, stage):
        sides = self.r.sides1 if stage == 0 else self.r.sides2
        for m in range(2):
            when(sides[1 - m].has)(self.rim_copy(stage, m).start)

    def fold(self, stage):
        r, q4, w, acc = self.r, self.q4, self.w, self.acc
        rows = r.rows_first == (stage == 0)
        sides = r.sides1 if stage == 0 else r.sides2
        for m in range(2):

            @when(sides[m].has)
            def _():
                self.rim_copy(stage, m).wait_recv()
                if rows:
                    cols = pl.ds(0, w) if stage == 0 else pl.ds(q4, 2 * q4)
                    rim = self.zr1 if stage == 0 else self.zr2
                    acc[1 + m, :, :, cols] = acc[1 + m, :, :, cols] + rim[m]
                else:
                    groups = pl.ds(0, 4) if stage == 0 else pl.ds(1, 2)
                    cols = pl.ds((1 + m) * q4, q4)
                    rim = self.xr1 if stage == 0 else self.xr2
                    acc[groups, :, :, cols] = acc[groups, :, :, cols] + rim[m]

    def share_copy(self, q):
        return remote(self.core.at[q], self.core.at[q], self.send.at[7], self.recv.at[7], self.partner)

    def share(self):
        q4 = self.q4
        self.core[self.r.q] = self.acc[1:3, :, :, q4 : 3 * q4]
        self.share_copy(self.r.q).start()

    def arrive(self):
        self.share_copy(self.r.o).wait_recv()

    def finish(self):
        r = self.r
        for i in range(3):
            self.pair_copy(i, not r.rows_first).wait_send()
        for m in range(2):
            when(r.sides1[1 - m].has)(self.rim_copy(0, m).wait_send)
            when(r.sides2[1 - m].has)(self.rim_copy(1, m).wait_send)
        self.share_copy(r.q).wait_send()


class ProbeSum:
    def __init__(self, role, mine, theirs, ppair, pacc, p1, pr1, pr2, total, send, recv, partner):
        self.r, self.mine, self.theirs = role, mine, theirs
        self.ppair, self.pacc, self.p1 = ppair, pacc, p1
        self.pr1, self.pr2, self.total = pr1, pr2, total
        self.send, self.recv, self.partner = send, recv, partner

    def copy(self, src, dst, stage, d, where):
        return remote(src, dst, self.send.at[stage, d], self.recv.at[stage, d], where)

    def pair_copy(self):
        return self.copy(self.theirs, self.ppair, 0, 0, self.partner)

    def begin(self):
        self.pair_copy().start()

    def scatter1(self):
        r = self.r
        out = []
        for d in range(1, r.n1):
            j = lax.rem(r.me1 + d, r.n1)
            src = self.pacc.at[pl.ds(j * r.n2, r.n2)]
            out.append(self.copy(src, self.pr1.at[pl.ds(d * r.n2, r.n2)], 1, d, {r.axis1: j}))
        return out

    def scatter2(self):
        r = self.r
        out = []
        for d in range(1, r.n2):
            j = lax.rem(r.me2 + d, r.n2)
            out.append(self.copy(self.p1.at[pl.ds(j, 1)], self.pr2.at[pl.ds(d, 1)], 2, d, {r.axis2: j}))
        return out

    def gather2(self, back):
        r = self.r
        out = []
        for d in range(1, r.n2):
            j = lax.rem(r.me2 + d, r.n2)
            origin = lax.rem(r.me2 - d + r.n2, r.n2) if back else r.me2
            ref = self.total.at[r.q, pl.ds(r.me1 * r.n2 + origin, 1)]
            out.append(self.copy(ref, ref, 3, d, {r.axis2: j}))
        return out

    def gather1(self, e, back):
        r = self.r
        out = []
        place = lax.rem(r.me2 - e + r.n2, r.n2)
        for d in range(1, r.n1):
            j = lax.rem(r.me1 + d, r.n1)
            origin = lax.rem(r.me1 - d + r.n1, r.n1) if back else r.me1
            ref = self.total.at[r.q, pl.ds(origin * r.n2 + place, 1)]
            out.append(self.copy(ref, ref, 5 + e, d, {r.axis1: j}))
        return out

    def share_copy(self, d, sender):
        r = self.r
        origin = lax.rem(r.me1 - d + r.n1, r.n1)
        ref = self.total.at[r.q, pl.ds(origin * r.n2, r.n2)]
        return self.copy(ref, ref, 4, d, self.partner)

    def step1(self):
        self.pair_copy().wait_recv()
        self.pacc[...] = self.mine[...] + self.ppair[...]
        for c in self.scatter1():
            c.start()

    def step2(self):
        r = self.r
        mine = self.pacc[pl.ds(r.me1 * r.n2, r.n2)]
        for d, c in enumerate(self.scatter1(), 1):
            c.wait_recv()
            mine = mine + self.pr1[d * r.n2 : (d + 1) * r.n2]
        self.p1[0 : r.n2] = mine
        for c in self.scatter2():
            c.start()

    def step3(self):
        r = self.r
        one = self.p1[pl.ds(r.me2, 1)]
        for d, c in enumerate(self.scatter2(), 1):
            c.wait_recv()
            one = one + self.pr2[d : d + 1]
        self.total[r.q, pl.ds(r.me1 * r.n2 + r.me2, 1)] = one
        for c in self.gather2(0) + self.gather1(0, 0):
            c.start()

    def step4(self):
        for e, c in enumerate(self.gather2(1), 1):
            c.wait_recv()
            for onward in self.gather1(e, 0):
                onward.start()
        self.share_copy(0, True).start()

    def step5(self):
        landing = [self.gather1(e, 1) for e in range(self.r.n2)]
        for d in range(1, self.r.n1):
            for e in range(self.r.n2):
                landing[e][d - 1].wait_recv()
            self.share_copy(d, True).start()

    def arrive(self):
        for d in range(self.r.n1):
            self.share_copy(d, False).wait_recv()

    def finish(self):
        self.pair_copy().wait_send()
        for c in self.scatter1() + self.scatter2() + self.gather2(0):
            c.wait_send()
        for e in range(self.r.n2):
            for c in self.gather1(e, 0):
                c.wait_send()
        for d in range(self.r.n1):
            self.share_copy(d, True).wait_send()


def line_greet(nx, ny, partner):
    mx, my = lax.axis_index("scanx"), lax.axis_index("scany")
    greet(
        [(True, partner)]
        + [(True, {"scanx": lax.rem(mx + d, nx)}) for d in range(1, nx)]
        + [(True, {"scany": lax.rem(my + d, ny)}) for d in range(1, ny)]
    )


def each(step):
    p = lax.axis_index("pos")
    for q in range(2):
        pl.when(p == q)(functools.partial(step, q))


def halo_kernel(nx, ny, spec, *refs):
    loaded, pad, kept = refs[:5], refs[5], refs[6:11]
    send, recv, local = refs[11:]
    tile = spec.shape[1]
    half = (pad.shape[1] - tile) // 2
    own = pl.ds(half, tile)
    partner = {"pos": 1 - lax.axis_index("pos")}
    loads = [pltpu.make_async_copy(spec, pad.at[:, own, own], local.at[0])]
    for i, (src, dst) in enumerate(zip(loaded, kept), 1):
        loads.append(pltpu.make_async_copy(src, dst, local.at[i]))
    for c in loads:
        c.start()
    roles = [Role(q, nx, ny) for q in range(2)]
    sides = roles[1].sides1 + roles[0].sides1
    greet([(True, partner)] + [(side.has, side.where) for side in sides])
    halos = [Halo(r, spec, pad, send, recv, partner) for r in roles]
    each(lambda q: halos[q].begin())
    for i, at in enumerate(
        (
            (slice(None), pl.ds(0, half)),
            (slice(None), pl.ds(half + tile, half)),
            (slice(None), slice(None), pl.ds(0, half)),
            (slice(None), slice(None), pl.ds(half + tile, half)),
        )
    ):

        @pl.when(jnp.logical_not(sides[i].has))
        def _(at=at):
            pad[at] = jnp.zeros(pad.at[at].shape, pad.dtype)

    def rest(q):
        halos[q].relay()
        halos[1 - q].arrive()
        halos[q].finish()

    each(rest)
    for c in loads:
        c.wait()


def step_kernel(offsets, pad, probe, amplitudes, table_a, table_b, grad, prob):
    m = probe.shape[1]
    tall, span = m + 8, m + 128
    pr, pi = probe[0], probe[1]
    grad[...] = jnp.zeros(grad.shape, grad.dtype)
    blank_rows = jnp.zeros((tall - m, m), jnp.float32)
    blank_cols = jnp.zeros((tall, span - m), jnp.float32)
    bf = jnp.bfloat16
    positions = amplitudes.shape[0]

    def place_at(j):
        row, col = offsets[j, 0], offsets[j, 1]
        row_in, col_in = lax.rem(row, 8), lax.rem(col, 128)
        rows = pl.ds(pl.multiple_of(row - row_in, 8), tall)
        cols = pl.ds(pl.multiple_of(col - col_in, 128), span)
        return row_in, col_in, rows, cols

    def place(j, k, term):
        row_in, col_in, rows, cols = place_at(j)
        moved = pltpu.roll(jnp.concatenate([term, blank_rows], 0), row_in, 0)
        moved = pltpu.roll(jnp.concatenate([moved, blank_cols], 1), col_in, 1)
        grad[k, rows, cols] = grad[k, rows, cols] + moved

    power = pr * pr + pi * pi
    for j in range(positions):
        place(j, 2, power)
    sum_r = sum_i = None
    for j in range(positions):
        row_in, col_in, rows, cols = place_at(j)

        def window(k):
            block = pad[k, rows, cols]
            block = pltpu.roll(block, lax.rem(span - col_in, span), 1)[:, :m]
            return pltpu.roll(block, lax.rem(tall - row_in, tall), 0)[:m]

        ar, ai = window(0), window(1)
        er = pr * ar - pi * ai
        ei = pr * ai + pi * ar
        left = dot(table_a[...], jnp.concatenate([er.astype(bf), ei.astype(bf)], 0)).astype(bf)
        far = dot(jnp.concatenate([left[:m], left[m:]], 1), table_b[...])
        fr, fi = far[:, :m], far[:, m:]
        ratio = amplitudes[j].astype(jnp.float32) / jnp.maximum(jnp.sqrt(fr * fr + fi * fi), 0.2)
        projected = jnp.concatenate([(fr * ratio).astype(bf), (fi * ratio).astype(bf)], 0)
        back_half = dot(table_b[...], projected).astype(bf)
        back = dot(jnp.concatenate([back_half[:m], back_half[m:]], 1), table_a[...])
        dr = back[:, :m] - er
        di = back[:, m:] - ei
        tr = ar * dr + ai * di
        ti = ar * di - ai * dr
        sum_r = tr if sum_r is None else sum_r + tr
        sum_i = ti if sum_i is None else sum_i + ti
        place(j, 0, pr * dr + pi * di)
        place(j, 1, pr * di - pi * dr)
    n, s, lanes = prob.shape[1:]
    for k, value in enumerate((sum_r, sum_i)):
        for c in range(n):
            r0, l0 = c * s % m, c * s // m * lanes
            prob[k, c] = value[r0 : r0 + s, l0 : l0 + lanes]


def reduce_kernel(nx, ny, *refs):
    grad, prob, core, icore, total = refs[:5]
    (pair, acc, xr1, xr2, zr1, zr2, ipair, iacc, ixr1, ixr2, izr1, izr2) = refs[5:17]
    (ppair, pacc, p1, pr1, pr2) = refs[17:22]
    (gsend, grecv, isend, irecv, psend, precv) = refs[22:]
    p = lax.axis_index("pos")
    partner = {"pos": 1 - p}
    line_greet(nx, ny, partner)
    roles = [Role(q, nx, ny) for q in range(2)]
    folds = [
        Fold(r, grad.at[r.q], grad.at[r.o], pair, acc, (xr1, xr2, zr1, zr2), core, gsend, grecv, partner)
        for r in roles
    ]
    lights = [
        Fold(
            r,
            grad.at[2, :, pl.ds(r.q, 1)],
            grad.at[2, :, pl.ds(r.o, 1)],
            ipair,
            iacc,
            (ixr1, ixr2, izr1, izr2),
            icore,
            isend,
            irecv,
            partner,
        )
        for r in roles
    ]
    probes = [
        ProbeSum(r, prob.at[r.q], prob.at[r.o], ppair, pacc, p1, pr1, pr2, total, psend, precv, partner)
        for r in roles
    ]

    def objects(q):
        probe_sum, fold, light = probes[q], folds[q], lights[q]
        probe_sum.begin()
        fold.begin()
        light.begin()
        probe_sum.step1()
        fold.add(0)
        fold.add(1)
        fold.send_rims(0)
        fold.add(2)
        for i in range(3):
            light.add(i)
        probe_sum.step2()
        light.send_rims(0)
        fold.fold(0)
        fold.send_rims(1)
        probe_sum.step3()
        light.fold(0)
        light.send_rims(1)
        probe_sum.step4()
        fold.fold(1)
        fold.share()
        light.fold(1)
        light.share()
        probe_sum.step5()
        light.arrive()
        fold.arrive()

    each(objects)
    def closing(q):
        probes[1 - q].arrive()
        lights[q].finish()
        folds[q].finish()
        probes[q].finish()

    each(closing)

def apply_kernel(step_size, core, light, total, pad, probe, new_spec, new_probe):
    tile = new_spec.shape[1]
    half = (pad.shape[1] - tile) // 2
    m = probe.shape[1]
    h = core.shape[3]
    for k in range(2):
        for g in range(2):
            for b in range(2):
                r0 = (2 * g + b) * h
                old = pad[k, half + r0 : half + r0 + h, half : half + tile]
                new_spec[k, r0 : r0 + h] = old + core[k, g, b] / (light[b, g, 0] + 1.0)
    n, s, lanes = total.shape[1:]
    for k in range(2):
        for c in range(n):
            rows = slice(c * s % m, c * s % m + s)
            cols = slice(c * s // m * lanes, c * s // m * lanes + lanes)
            new_probe[k, rows, cols] = probe[k, rows, cols] + total[k, c] * step_size


def tables(length):
    index = np.arange(length)
    angle = ((index[:, None] * index[None, :]) % length).astype(np.float32) * np.float32(2.0 * math.pi / length)
    scale = np.float32(1.0 / math.sqrt(length))
    c = np.cos(angle) * scale
    s = np.sin(angle) * scale
    a = np.block([[c, s], [-s, c]]).astype(jnp.bfloat16)
    b = np.block([[c, -s], [s, c]]).astype(jnp.bfloat16)
    return a, b


def shards(nx, ny, consts, specimen, probe_wave, amplitudes, offsets):
    m = probe_wave.shape[1]
    tile = specimen.shape[1]
    wide = tile + m
    f32 = jnp.float32
    vm = pl.BlockSpec(memory_space=VMEM)
    sm = pl.BlockSpec(memory_space=pltpu.SMEM)
    anywhere = pl.BlockSpec(memory_space=pl.ANY)
    dma = pltpu.SemaphoreType.DMA
    lanes = 128
    n = nx * ny
    s = m * m // lanes // n
    h = wide // 8
    most = max(nx, ny)
    positions = offsets.shape[0]
    shaped = VMEM
    held = (offsets, probe_wave, amplitudes, consts[0], consts[1])
    hbm = pl.BlockSpec(memory_space=pltpu.HBM)
    pad, *held = pl.pallas_call(
        functools.partial(halo_kernel, nx, ny),
        out_shape=[shaped((2, wide, wide), f32)] + [shaped(x.shape, x.dtype) for x in held],
        in_specs=[hbm] * 6,
        out_specs=[vm] * 6,
        scratch_shapes=[dma((16,)), dma((16,)), dma((6,))],
        compiler_params=pltpu.CompilerParams(vmem_limit_bytes=16 * 2**20, collective_id=0, has_side_effects=True),
        name="halo",
    )(*[pltpu.with_memory_space_constraint(x, pltpu.HBM) for x in (specimen, *held)])
    grad, prob = pl.pallas_call(
        step_kernel,
        out_shape=[
            jax.ShapeDtypeStruct((3, wide, wide), f32),
            jax.ShapeDtypeStruct((2, n, s, lanes), f32),
        ],
        in_specs=[sm] + [vm] * 5,
        out_specs=[vm, vm],
        compiler_params=pltpu.CompilerParams(vmem_limit_bytes=32 * 2**20),
        name="step",
    )(held[0], pad, *held[1:])

    def field(size):
        return [
            VMEM((4, size, h, wide), f32),
            VMEM((4, size, h, wide), f32),
            VMEM((2, 4, size, h, wide // 4), f32),
            VMEM((2, 2, size, h, wide // 4), f32),
            VMEM((2, size, h, wide), f32),
            VMEM((2, size, h, wide // 2), f32),
        ]

    step_size = 1.0 / math.sqrt(positions * n * 2)
    core, light, total = pl.pallas_call(
        functools.partial(reduce_kernel, nx, ny),
        out_shape=[
            shaped((2, 2, 2, h, wide // 2), f32),
            shaped((2, 2, 1, h, wide // 2), f32),
            shaped((2, n, s, lanes), f32),
        ],
        in_specs=[vm] * 2,
        out_specs=[vm, vm, vm],
        scratch_shapes=[
            *field(2),
            *field(1),
            VMEM((n, s, lanes), f32),
            VMEM((n, s, lanes), f32),
            VMEM((most, s, lanes), f32),
            VMEM((n, s, lanes), f32),
            VMEM((most, s, lanes), f32),
            dma((8,)),
            dma((8,)),
            dma((8,)),
            dma((8,)),
            dma((5 + most, most)),
            dma((5 + most, most)),
        ],
        compiler_params=pltpu.CompilerParams(vmem_limit_bytes=32 * 2**20, collective_id=1, has_side_effects=True),
        name="reduce",
    )(grad.reshape(3, 4, 2, h, wide), prob)
    return pl.pallas_call(
        functools.partial(apply_kernel, step_size),
        out_shape=[
            jax.ShapeDtypeStruct(specimen.shape, f32),
            jax.ShapeDtypeStruct(probe_wave.shape, f32),
        ],
        in_specs=[vm] * 5,
        out_specs=[vm, vm],
        compiler_params=pltpu.CompilerParams(vmem_limit_bytes=16 * 2**20),
        name="apply",
    )(core, light, total, pad, held[1])


def solution(mesh):
    nx, ny = mesh.shape["scanx"], mesh.shape["scany"]

    def run(specimen, probe_wave, amplitudes, offsets):
        consts = tables(probe_wave.shape[2])
        return jax.shard_map(
            lambda *args: shards(nx, ny, [jnp.asarray(t) for t in consts], *args),
            mesh=mesh,
            in_specs=(
                P(None, ("groups", "scanx"), "scany"),
                P(None, "groups", None),
                P(("groups", "scanx", "scany", "pos"), None, None),
                P(("groups", "scanx", "scany", "pos"), None),
            ),
            out_specs=(P(None, ("groups", "scanx"), "scany"), P(None, "groups", None)),
            check_vma=False,
        )(specimen, probe_wave, amplitudes, offsets)

    return run
```
